32 devices in a mesh: gx: 4 (over y, core), gy: 4 (over z), gz: 2 (over x).
Axes of the slice: x: 2, y: 2, z: 4, core: 2. Of those that a mesh axis runs over, the one named last changes fastest.
Arguments:
- gas_state: float32 [5, 32, 64, 256], P(None, 'gx', 'gy', 'gz'), may hold values from -6 to 6, as said below
- section_start: float32 [5, 32, 64, 256], P(None, 'gx', 'gy', 'gz'), may hold values from -6 to 6
- drop_cell: int32 [4, 4, 2, 16, 128], P('gx', 'gy', 'gz'), may hold values from 0 to 8191
- block_tile: int32 [4, 4, 2, 16], P('gx', 'gy', 'gz'), may hold values from 0 to 1, as said below
- droplets_per_block: int32 [4, 4, 2, 16], P('gx', 'gy', 'gz'), may hold values from 0 to 128, as said below
- drop_frac: float32 [4, 4, 2, 3, 16, 128], P('gx', 'gy', 'gz'), may hold values from -0.5 to 0.5
- drop_vel: float32 [4, 4, 2, 3, 16, 128], P('gx', 'gy', 'gz'), may hold values from -6 to 6
- drop_mass: float32 [4, 4, 2, 16, 128], P('gx', 'gy', 'gz'), may hold values from 0.1 to 4
- drop_temp: float32 [4, 4, 2, 16, 128], P('gx', 'gy', 'gz'), may hold values from -6 to 6
Outputs:
- new_state: float32 [5, 32, 64, 256], P(None, 'gx', 'gy', 'gz')
The draws below stay inside these ranges and needn't reach their ends.
Inputs may be any that keep to these rules, and one draw needn't show every extreme that they name: `gas_state`: component 0 (density) lies between 0.3 and 3.4. `drop_cell`: encodes the cell (x, y, z) within the block's tile as (x * 8 + y) * 128 + z. `block_tile`: nondecreasing along a device's blocks; blocks with count 0 carry tile 1 (the last tile). `droplets_per_block`: on each device the blocks with a positive count come first and every later block has count 0; each device has at least 4 live blocks, one of them with 128 droplets; some device has all 16 blocks live. Slot d of a block is live when d is below its count.
All inputs are finite; a program needn't handle non-finite values.
Results may differ from the reference program's by a relative error of at most 0.00057.
Values sent between devices are 32-bit elements; how exact they have to be, the bound alone decides.
A program may use at most 64 MiB of HBM per device.

```python
import math
import jax
import jax.numpy as jnp
from jax import lax

CX = 8
CY = 16
CZ = 128
TS = 8
BLK = 128
NBLK = 16
NTILE = 2
NX = 32
NY = 64
NZ = 256
N_GX = 4
N_GY = 4
N_GZ = 2


def draw_gas_state(key, part):
    first_key, second_key = jax.random.split(jax.random.fold_in(key, 11))
    flow_shape = (4, NX, NY, NZ)
    velocity_temp = jnp.clip(jax.random.normal(second_key, flow_shape, jnp.float32), -6.0, 6.0)
    density = jnp.exp(0.3 * jnp.clip(jax.random.normal(first_key, (1, NX, NY, NZ), jnp.float32), -4.0, 4.0))
    return jnp.concatenate([density, velocity_temp], axis=0)


def block_layout(key):
    key_list = jax.random.split(jax.random.fold_in(key, 5), 6)
    devices = N_GX * N_GY * N_GZ
    span_size = NBLK - NBLK // 4
    first_draw = jax.random.randint(key_list[0], (devices,), 0, span_size + 1)
    second_draw = jax.random.randint(key_list[1], (devices,), 0, span_size + 1)
    live_blocks = NBLK // 4 + first_draw * second_draw // max(span_size, 1)
    chosen = jax.random.randint(key_list[2], (), 0, devices)
    live_blocks = jnp.where(jnp.arange(devices) == chosen, NBLK, live_blocks)
    positions = jnp.arange(NBLK, dtype=jnp.int32)[None, :]
    counts = jax.random.randint(key_list[3], (devices, NBLK), max(BLK // 2, 1), BLK + 1)
    full_block = jax.random.randint(key_list[4], (devices,), 0, live_blocks)
    counts = jnp.where(positions == full_block[:, None], BLK, counts)
    counts = jnp.where(positions < live_blocks[:, None], counts, 0)
    tile_ids = jax.random.randint(key_list[5], (devices, NBLK), 0, NTILE)
    tile_ids = jnp.where(positions < live_blocks[:, None], tile_ids, NTILE - 1)
    tile_ids = jnp.sort(tile_ids, axis=1)
    return (counts.reshape(N_GX, N_GY, N_GZ, NBLK).astype(jnp.int32), tile_ids.reshape(N_GX, N_GY, N_GZ, NBLK).astype(jnp.int32))


def draw_droplets_per_block(key, part):
    return block_layout(key)[0]


def draw_block_tile(key, part):
    return block_layout(key)[1]


def with_ends(entries, rng, smallest, largest):
    longest = entries.shape.index(max(entries.shape))
    spots = []
    for shift in (0, 1):
        where = [jax.random.randint(jax.random.fold_in(rng, axis), (), 0, length) for axis, length in enumerate(entries.shape)]
        where[longest] = (where[longest] + shift) % entries.shape[longest]
        spots.append(tuple(where))
    return entries.at[spots[0]].set(smallest).at[spots[1]].set(largest)


def block_levels(key, extent, pieces, smallest, top_value):
    loudness = 1.0
    for axis_at, shards_of in pieces:
        draws = jax.random.uniform(jax.random.fold_in(jax.random.fold_in(key, 6), axis_at), (shards_of,), jnp.float32, smallest / len(pieces), top_value / len(pieces))
        loudness = loudness * jnp.repeat(jnp.exp(draws), extent[axis_at] // shards_of).reshape((-1,) + (1,) * (len(extent) - 1 - axis_at))
    return loudness


def bell_draw(stream_key, shape, deviation, reach, cuts=(), held_as=jnp.bfloat16):
    loudness = block_levels(stream_key, shape, cuts, -0.22, 0.18) if cuts else 1.0
    values = jax.random.normal(stream_key, shape, jnp.float32) * deviation * loudness
    return jnp.minimum(jnp.maximum(values, -reach), reach).astype(held_as)


def setup_inputs(seed: int = 0) -> dict:
    keys = jax.random.split(jax.random.key(seed), 10)
    return {
        "gas_state": draw_gas_state(jax.random.fold_in(keys[9], 71), 0),
        "section_start": bell_draw(keys[1], (5, NX, NY, NZ), 1.0, 6.0, ((1, 4), (2, 4), (3, 2)), jnp.float32),
        "drop_cell": with_ends(jax.random.randint(keys[2], (N_GX, N_GY, N_GZ, NBLK, BLK), 0, TS * TS * CZ), jax.random.fold_in(keys[2], 1), 0, (TS * TS * CZ) - 1).astype(jnp.int32),
        "block_tile": draw_block_tile(jax.random.fold_in(keys[9], 71), 0),
        "droplets_per_block": draw_droplets_per_block(jax.random.fold_in(keys[9], 71), 0),
        "drop_frac": jnp.clip(jax.random.uniform(keys[5], (N_GX, N_GY, N_GZ, 3, NBLK, BLK), jnp.float32, -0.5, 0.5) * block_levels(keys[5], (N_GX, N_GY, N_GZ, 3, NBLK, BLK), ((0, 4), (1, 4), (2, 2)), -0.4, 0.0), -0.5, 0.5),
        "drop_vel": bell_draw(keys[6], (N_GX, N_GY, N_GZ, 3, NBLK, BLK), 1.0, 6.0, ((0, 4), (1, 4), (2, 2)), jnp.float32),
        "drop_mass": jnp.clip(jnp.exp(math.log(4.0) - 3.6888794 * jax.random.uniform(keys[7], (N_GX, N_GY, N_GZ, NBLK, BLK), jnp.float32) ** block_levels(keys[7], (N_GX, N_GY, N_GZ, NBLK, BLK), ((0, 4), (1, 4), (2, 2)), -0.2, 0.2)), 0.1, 4.0),
        "drop_temp": bell_draw(keys[8], (N_GX, N_GY, N_GZ, NBLK, BLK), 1.0, 6.0, ((0, 4), (1, 4), (2, 2)), jnp.float32),
    }


PARCEL = 8.0
LATENT = 0.5
TIME_INCREMENT = 0.2
VISCOSITY = 0.5


def cut_windows(values, tile_size):
    number = (values.shape[0] - 2) // tile_size
    trailing = values.shape[1:]
    rest_pad = [(0, 0)] * len(trailing)
    leading = values[:number * tile_size].reshape((number, tile_size) + trailing)
    upper_rows = jnp.pad(values[tile_size:], [(0, tile_size - 2)] + rest_pad)
    upper_rows = upper_rows.reshape((number, tile_size) + trailing)[:, :2]
    return jnp.concatenate([leading, upper_rows], axis=1)


def join_windows(values, tile_size):
    number = values.shape[0]
    trailing = values.shape[2:]
    rest_pad = [(0, 0)] * len(trailing)
    leading = values[:, :tile_size].reshape((number * tile_size,) + trailing)
    leading = jnp.pad(leading, [(0, 2)] + rest_pad)
    upper_rows = jnp.pad(values[:, tile_size:], [(0, 0), (0, tile_size - 2)] + rest_pad)
    upper_rows = upper_rows.reshape((number * tile_size,) + trailing)
    upper_rows = jnp.pad(upper_rows, [(tile_size, 0)] + rest_pad)[:number * tile_size + 2]
    return leading + upper_rows


def tile_footprints(padded, tile_size):
    arranged = cut_windows(jnp.moveaxis(padded, 1, 0), tile_size)
    arranged = cut_windows(jnp.moveaxis(arranged, 3, 0), tile_size)
    arranged = jnp.transpose(arranged, (2, 0, 4, 3, 1, 5))
    return arranged.reshape(arranged.shape[0] * arranged.shape[1], -1, arranged.shape[5])


def tiles_to_padded(tile_sums, tiles_x, tile_rows_along_y, components, tile_size):
    foot_width = tile_size + 2
    arranged = tile_sums.reshape(tiles_x, tile_rows_along_y, components, foot_width, foot_width, tile_sums.shape[2])
    arranged = jnp.transpose(arranged, (0, 3, 1, 4, 2, 5))
    arranged = join_windows(arranged, tile_size)
    arranged = join_windows(jnp.moveaxis(arranged, 0, 2), tile_size)
    return jnp.transpose(arranged, (2, 1, 0, 3))


def spread(position, offset, length):
    places = jnp.arange(length, dtype=jnp.int32)[None, :, None]
    anchor = position[:, None, :]
    low_weight = (0.5 * (0.5 - offset) * (0.5 - offset))[:, None, :]
    middle = (0.75 - offset * offset)[:, None, :]
    higher = (0.5 * (0.5 + offset) * (0.5 + offset))[:, None, :]
    return (jnp.where(places == anchor, low_weight, 0.0) + jnp.where(places == anchor + 1, middle, 0.0)
            + jnp.where(places == anchor + 2, higher, 0.0))


def block_weights(drop_cells, offsets, tile_size, cells_z):
    plane_size = tile_size * cells_z
    pos_x = drop_cells // plane_size
    pos_y = (drop_cells // cells_z) % tile_size
    pos_z = drop_cells % cells_z
    foot_width = tile_size + 2
    weight_x = spread(pos_x, offsets[0], foot_width)
    weight_y = spread(pos_y, offsets[1], foot_width)
    planar = (weight_x[:, :, None, :] * weight_y[:, None, :, :]).reshape(
        drop_cells.shape[0], foot_width * foot_width, drop_cells.shape[1])
    upward_direction = spread(pos_z, offsets[2], cells_z + 2)
    return planar, upward_direction


def droplet_terms(gas_at, velocity, masses, temper, counts):
    slots = jnp.arange(masses.shape[1], dtype=jnp.int32)[None, :]
    alive_weight = jnp.where(slots < counts[:, None], PARCEL, 0.0)
    diameter = jnp.cbrt(masses)
    spalding = jax.nn.softplus(gas_at[:, 4] - temper)
    evaporation = diameter * jnp.log1p(spalding)
    drag_force = (diameter * gas_at[:, 0])[:, None, :] * (gas_at[:, 1:4] - velocity)
    heat_flux = diameter * (gas_at[:, 4] - temper)
    momentum = evaporation[:, None, :] * velocity - drag_force
    energy = -heat_flux - LATENT * evaporation
    stacked = jnp.concatenate([evaporation[:, None, :], momentum, energy[:, None, :]], axis=1)
    return stacked * alive_weight[:, None, :]


def device_sources(footprints, drop_cells, tile_ids, counts, offsets, velocity, masses, temper):
    blocks, block_size = drop_cells.shape
    planar, upward_direction = block_weights(drop_cells, offsets, TS, CZ)
    planar = lax.optimization_barrier(planar.astype(jnp.bfloat16)).astype(jnp.float32)
    upward_direction = lax.optimization_barrier(upward_direction.astype(jnp.bfloat16)).astype(jnp.float32)
    source_portions = jnp.take(footprints, tile_ids, axis=0).astype(jnp.float32)
    nearby_gas_values = jnp.einsum("gsy,gyn->gsn", source_portions, upward_direction)
    gas_at = jnp.sum(nearby_gas_values.reshape(blocks, 5, -1, block_size) * planar[:, None], axis=2)
    sources = droplet_terms(gas_at, jnp.transpose(velocity, (1, 0, 2)), masses, temper, counts)
    weight_scaled_terms = (planar[:, None] * sources[:, :, None, :]).astype(jnp.bfloat16)
    weight_scaled_terms = lax.optimization_barrier(weight_scaled_terms).astype(jnp.float32).reshape(blocks, -1, block_size)
    spread_sources = jnp.einsum("peh,pch->pec", weight_scaled_terms, upward_direction)
    owners = (tile_ids[:, None] == jnp.arange(footprints.shape[0], dtype=jnp.int32)[None, :]).astype(jnp.float32)
    return jnp.einsum("bt,bkz->tkz", owners, spread_sources, precision=lax.Precision.HIGHEST)


def neighbour(padded, dim_index, offset):
    slicer = [slice(None), slice(1, -1), slice(1, -1), slice(1, -1)]
    length = padded.shape[dim_index] - 2
    slicer[dim_index] = slice(1 + offset, 1 + offset + length)
    return padded[tuple(slicer)]


def advance(padded, gas_state, section_start, sources):
    laplace = -6.0 * gas_state
    advect = jnp.zeros_like(gas_state)
    for dim_index in (1, 2, 3):
        higher = neighbour(padded, dim_index, 1)
        lower_cells = neighbour(padded, dim_index, -1)
        laplace = laplace + higher + lower_cells
        advect = advect + gas_state[dim_index][None] * (higher - lower_cells) * 0.5
    return 0.75 * section_start + 0.25 * (gas_state + TIME_INCREMENT * (VISCOSITY * laplace - advect + sources))


def reference(gas_state, section_start, drop_cell, block_tile, droplets_per_block, drop_frac, drop_vel, drop_mass, drop_temp):
    padded = jnp.pad(gas_state, ((0, 0), (1, 1), (1, 1), (1, 1)), mode="wrap")
    rounded = lax.optimization_barrier(padded.astype(jnp.bfloat16))
    devices = N_GX * N_GY * N_GZ

    def flatten(values):
        return values.reshape((devices,) + values.shape[3:])

    inputs = (flatten(drop_cell), flatten(block_tile), flatten(droplets_per_block), flatten(drop_frac),
              flatten(drop_vel), flatten(drop_mass), flatten(drop_temp), jnp.arange(devices, dtype=jnp.int32))
    running = jnp.zeros((5, NX + 2, NY + 2, NZ + 2), jnp.float32)

    def deposit_device(running, device_item):
        drop_cells, tile_ids, counts, offsets, velocity, masses, temper, device = device_item
        corner_x = ((device // (N_GY * N_GZ)) * CX).astype(jnp.int32)
        corner_y = (((device // N_GZ) % N_GY) * CY).astype(jnp.int32)
        corner_z = ((device % N_GZ) * CZ).astype(jnp.int32)
        root = (jnp.zeros((), jnp.int32), corner_x, corner_y, corner_z)
        local_cells = lax.dynamic_slice(rounded, root, (5, CX + 2, CY + 2, CZ + 2))
        footprints = tile_footprints(local_cells, TS)
        tile_sums = device_sources(footprints, drop_cells, tile_ids, counts, offsets, velocity, masses, temper)
        spread_sources = tiles_to_padded(tile_sums, CX // TS, CY // TS, 5, TS)
        current = lax.dynamic_slice(running, root, spread_sources.shape)
        return lax.dynamic_update_slice(running, current + spread_sources, root), None

    running, ignored = lax.scan(deposit_device, running, inputs)
    for dim_index in (1, 2, 3):
        moved_axis = jnp.moveaxis(running, dim_index, 0)
        core_cells = moved_axis[1:-1].at[0].add(moved_axis[-1]).at[-1].add(moved_axis[0])
        running = jnp.moveaxis(core_cells, 0, dim_index)
    return advance(padded, gas_state, section_start, running)
```

```python
import functools

import jax
import jax.numpy as jnp
from jax import lax
from jax.experimental import pallas as pl
from jax.experimental.pallas import tpu as pltpu
from jax.sharding import PartitionSpec as P

TS = 8
PARCEL = 8.0
LATENT = 0.5
TIME_INCREMENT = 0.2
VISCOSITY = 0.5
MESH = pl.DeviceIdType.MESH
LANES = 128
F32 = jnp.float32
BF16 = jnp.bfloat16

DIRS = ((-1, 0), (1, 0), (0, -1), (0, 1), (-1, -1), (-1, 1), (1, -1), (1, 1))
OPPOSITE = (1, 0, 3, 2, 7, 6, 5, 4)


def int_div(values, number):
    if number & (number - 1) == 0:
        return lax.shift_right_logical(values, jnp.int32(number.bit_length() - 1))
    return lax.div(values, jnp.int32(number))


def int_mod(values, number):
    if number & (number - 1) == 0:
        return values & jnp.int32(number - 1)
    return lax.rem(values, jnp.int32(number))


def tap(places, anchor, low, middle, high):
    return jnp.where(
        places == anchor,
        low,
        jnp.where(places == anchor + 1, middle, jnp.where(places == anchor + 2, high, 0.0)),
    )


def kernel(
    tile_ref,
    count_ref,
    gas_ref,
    cell_ref,
    frac_ref,
    vel_ref,
    mass_ref,
    temp_ref,
    out_ref,
    weight_ref,
    planar_ref,
    vert_ref,
    vghost_ref,
    scaled_ref,
    sghost_ref,
    lhs_ref,
    ghost_ref,
    ysend_ref,
    csend_ref,
    crecv_ref,
    zsend_ref,
    zrecv_ref,
    gasat_ref,
    source_ref,
    dep_ref,
    dcsend_ref,
    dzsend_ref,
    dzrecv_ref,
    dxrecv_ref,
    dyrecv_ref,
    dcrecv_ref,
    send_sem,
    recv_sem,
):
    comps, cx, cy, cz = gas_ref.shape
    blocks, slots = cell_ref.shape
    plane = cx * cy
    starts = (0, cy, 2 * cy, 2 * cy + cx)
    sizes = (cy, cy, cx, cx)
    corner_at = 2 * cy + 2 * cx
    width = lhs_ref.shape[1]
    used = dep_ref.shape[1]

    ix, iy, iz = lax.axis_index("gx"), lax.axis_index("gy"), lax.axis_index("gz")
    nx, ny, nz = lax.axis_size("gx"), lax.axis_size("gy"), lax.axis_size("gz")

    def xy_id(k):
        dx, dy = DIRS[k]
        return {"gx": lax.rem(ix + dx + nx, nx), "gy": lax.rem(iy + dy + ny, ny), "gz": iz}

    def z_id(side):
        return {"gx": ix, "gy": iy, "gz": lax.rem(iz + (2 * side - 1) + nz, nz)}

    barrier = pltpu.get_barrier_semaphore()
    for k in range(8):
        pl.semaphore_signal(barrier, inc=1, device_id=xy_id(k), device_id_type=MESH)
    for side in range(2):
        pl.semaphore_signal(barrier, inc=1, device_id=z_id(side), device_id_type=MESH)

    csend_ref[...] = jnp.zeros_like(csend_ref)
    zsend_ref[...] = jnp.zeros_like(zsend_ref)
    ghost_ref[:, corner_at:, :] = jnp.zeros(
        (comps, ghost_ref.shape[1] - corner_at, cz), F32
    )
    ysend_ref[0] = gas_ref[:, :, 0, :]
    ysend_ref[1] = gas_ref[:, :, cy - 1, :]
    for j in range(4):
        dx, dy = DIRS[4 + j]
        csend_ref[j, :comps, :] = gas_ref[:, 0 if dx < 0 else cx - 1, 0 if dy < 0 else cy - 1, :]

    pl.semaphore_wait(barrier, 10)

    def xy_copy(k, base, src, dst):
        return pltpu.make_async_remote_copy(
            src_ref=src,
            dst_ref=dst,
            send_sem=send_sem.at[base + k],
            recv_sem=recv_sem.at[base + OPPOSITE[k]],
            device_id=xy_id(k),
            device_id_type=MESH,
        )

    halo = []
    for k in (4, 5, 6, 7, 0, 1, 2, 3):
        other = OPPOSITE[k]
        if k < 2:
            src = gas_ref.at[:, 0 if k == 0 else cx - 1]
        elif k < 4:
            src = ysend_ref.at[k - 2]
        else:
            src = csend_ref.at[k - 4]
        if k < 4:
            dst = ghost_ref.at[:, pl.ds(starts[other], sizes[other])]
        else:
            dst = crecv_ref.at[other - 4]
        copy = xy_copy(k, 0, src, dst)
        copy.start()
        halo.append(copy)

    cells = cell_ref[...]
    weight_ref[0] = int_div(cells, TS * cz).astype(F32)
    weight_ref[1] = int_mod(int_div(cells, cz), TS).astype(F32)
    weight_ref[2] = int_mod(cells, cz).astype(F32)
    for axis in range(3):
        offset = frac_ref[axis]
        weight_ref[3 + 3 * axis] = 0.5 * (0.5 - offset) * (0.5 - offset)
        weight_ref[4 + 3 * axis] = 0.75 - offset * offset
        weight_ref[5 + 3 * axis] = 0.5 * (0.5 + offset) * (0.5 + offset)

    tiles_y = cy // TS

    def lane_block(b):
        return pl.ds(pl.multiple_of(b * slots, slots), slots)

    def places(rows, first):
        return (lax.broadcasted_iota(jnp.int32, (rows, slots), 0) + first).astype(F32)

    def ends(length):
        row = lax.broadcasted_iota(jnp.int32, (8, slots), 0)
        return jnp.where(row == 0, 0, jnp.where(row == 1, length + 1, -8)).astype(F32)

    def make_weights(b, carry):
        def row(i):
            return weight_ref[i, pl.ds(b, 1), :]

        tile = tile_ref[b]
        corner_x = (int_div(tile, tiles_y) * TS).astype(F32)
        corner_y = (int_mod(tile, tiles_y) * TS).astype(F32)
        anchor_x, anchor_y, anchor_z = row(0) + corner_x, row(1) + corner_y, row(2)
        tx, ty, tz = [tuple(row(3 + 3 * a + i) for i in range(3)) for a in range(3)]
        wx, wxe = tap(places(cx, 1), anchor_x, *tx), tap(ends(cx), anchor_x, *tx)
        wy, wye = tap(places(cy, 1), anchor_y, *ty), tap(ends(cy), anchor_y, *ty)
        corners = [
            wxe[0 if dx < 0 else 1][None] * wye[0 if dy < 0 else 1][None] for dx, dy in DIRS[4:]
        ]
        planar = jnp.concatenate(
            [
                (wx[:, None, :] * wy[None, :, :]).reshape(plane, slots),
                wxe[0:1] * wy,
                wxe[1:2] * wy,
                wx * wye[0:1],
                wx * wye[1:2],
            ]
            + corners
            + [jnp.zeros((width - plane - corner_at - 4, slots), F32)],
            axis=0,
        )
        at = lane_block(b)
        planar_ref[:, at] = planar.astype(BF16)
        vert_ref[:, at] = tap(places(cz, 1), anchor_z, *tz).astype(BF16)
        vghost_ref[b] = tap(ends(cz), anchor_z, *tz).astype(BF16).astype(F32)
        return carry

    lax.fori_loop(0, blocks, make_weights, 0)

    for c in range(comps):
        turned = gas_ref[c].reshape(plane, cz).T
        lhs_ref[c * cz : (c + 1) * cz, :plane] = turned.astype(BF16)
        zsend_ref[0, c : c + 1, :plane] = turned[0:1]
        zsend_ref[1, c : c + 1, :plane] = turned[cz - 1 : cz]

    for copy in halo:
        copy.wait_recv()

    for c in range(comps):
        ghost_ref[c, corner_at : corner_at + 4, :] = crecv_ref[:, c, :]
        turned = ghost_ref[c].T
        lhs_ref[c * cz : (c + 1) * cz, plane:] = turned.astype(BF16)
        zsend_ref[0, c : c + 1, plane:] = turned[0:1]
        zsend_ref[1, c : c + 1, plane:] = turned[cz - 1 : cz]

    def z_copy(side, base, src, dst):
        return pltpu.make_async_remote_copy(
            src_ref=src.at[side],
            dst_ref=dst.at[1 - side],
            send_sem=send_sem.at[base + side],
            recv_sem=recv_sem.at[base + 1 - side],
            device_id=z_id(side),
            device_id_type=MESH,
        )

    z_halo = [z_copy(side, 8, zsend_ref, zrecv_ref) for side in range(2)]
    for copy in z_halo:
        copy.start()

    pair = 2 if blocks % 2 == 0 else 1

    def gather(i, carry):
        at = pl.ds(pl.multiple_of(i * pair * slots, pair * slots), pair * slots)
        planar = planar_ref[:, at]
        vertical = vert_ref[:, at].astype(F32)
        for c in range(comps):
            near = jnp.dot(
                lhs_ref[c * cz : (c + 1) * cz, :], planar, preferred_element_type=F32
            )
            value = jnp.sum(near * vertical, axis=0, keepdims=True)
            for j in range(pair):
                gasat_ref[c, pl.ds(i * pair + j, 1), :] = value[:, j * slots : (j + 1) * slots]
        return carry

    lax.fori_loop(0, blocks // pair, gather, 0)

    for copy in z_halo:
        copy.wait_recv()

    z_values = jnp.concatenate([zrecv_ref[0], zrecv_ref[1]], axis=0).astype(BF16)
    near_ends = jnp.dot(z_values, planar_ref[...], preferred_element_type=F32)
    for b in range(blocks):
        part = near_ends[:, b * slots : (b + 1) * slots]
        both = part[:8] * vghost_ref[b, 0:1, :] + part[8:] * vghost_ref[b, 1:2, :]
        for c in range(comps):
            gasat_ref[c, b : b + 1, :] += both[c : c + 1]

    temper = temp_ref[...]
    diameter = jnp.exp(jnp.log(mass_ref[...]) * (1.0 / 3.0))
    excess = gasat_ref[4] - temper
    spalding = jnp.maximum(excess, 0.0) + jnp.log1p(jnp.exp(-jnp.abs(excess)))
    rate = diameter * jnp.log1p(spalding)
    drag = diameter * gasat_ref[0]
    heat = diameter * excess
    source_ref[0] = rate
    for a in range(3):
        velocity = vel_ref[a]
        source_ref[1 + a] = rate * velocity - drag * (gasat_ref[1 + a] - velocity)
    source_ref[4] = -heat - LATENT * rate

    sghost_ref[...] = jnp.zeros_like(sghost_ref)
    slot_ids = lax.broadcasted_iota(jnp.int32, (1, slots), 1)

    def scale(b, carry):
        at = lane_block(b)
        alive = jnp.where(slot_ids < count_ref[b], PARCEL, 0.0)
        vertical = vert_ref[:, at].astype(F32)
        low, high = vghost_ref[b, 0:1, :], vghost_ref[b, 1:2, :]
        rows = []
        for c in range(comps):
            strength = source_ref[c, pl.ds(b, 1), :] * alive
            scaled_ref[c * cz : (c + 1) * cz, at] = (vertical * strength).astype(BF16)
            rows.append(strength)
        strengths = jnp.concatenate(rows + [jnp.zeros((8 - comps, slots), F32)], axis=0)
        sghost_ref[:, at] = jnp.concatenate([strengths * low, strengths * high], axis=0).astype(BF16)
        return carry

    lax.fori_loop(0, blocks, scale, 0)

    def contract(lhs, rhs):
        return lax.dot_general(lhs, rhs, (((1,), (1,)), ((), ())), preferred_element_type=F32)

    z_ends = contract(sghost_ref[...], planar_ref[...])
    dzsend_ref[0] = z_ends[:8]
    dzsend_ref[1] = z_ends[8:]
    z_deposit = [z_copy(side, 10, dzsend_ref, dzrecv_ref) for side in range(2)]
    for copy in z_deposit:
        copy.start()

    for c in range(comps):
        dep_ref[c] = contract(planar_ref[:used, :], scaled_ref[c * cz : (c + 1) * cz, :])

    for copy in z_deposit:
        copy.wait_recv()

    lane = lax.broadcasted_iota(jnp.int32, (plane, cz), 1)
    row_y = int_mod(lax.broadcasted_iota(jnp.int32, (plane, cz), 0), cy)

    def columns(ref, first):
        both = jnp.concatenate([ref[0], ref[1]], axis=0)[:, first : first + LANES]
        return jnp.concatenate([both, jnp.zeros((LANES - 16, LANES), F32)], axis=0).T

    def at_ends(turned, rows, c):
        lanes = lax.broadcasted_iota(jnp.int32, (rows, cz), 1)
        low, high = turned[:rows, c : c + 1], turned[:rows, 8 + c : 9 + c]
        return jnp.where(lanes == 0, low, 0.0) + jnp.where(lanes == cz - 1, high, 0.0)

    outer = columns(dzrecv_ref, plane)
    dcsend_ref[...] = jnp.zeros_like(dcsend_ref)
    for c in range(comps):
        dep_ref[c, plane:, :] += at_ends(outer, used - plane, c)
        for j in range(4):
            dcsend_ref[j, c : c + 1, :] = dep_ref[c, plane + corner_at + j : plane + corner_at + j + 1, :]

    deposit = []
    for k in (4, 5, 6, 7, 0, 1, 2, 3):
        other = OPPOSITE[k]
        if k < 4:
            src = dep_ref.at[:, pl.ds(plane + starts[k], sizes[k])]
            dst = (dxrecv_ref if k < 2 else dyrecv_ref).at[other % 2]
        else:
            src, dst = dcsend_ref.at[k - 4], dcrecv_ref.at[other - 4]
        copy = xy_copy(k, 12, src, dst)
        copy.start()
        deposit.append(copy)

    inner = columns(dzrecv_ref, 0)
    z_sides = columns(zrecv_ref, 0)
    flow = [gas_ref[1 + a].reshape(plane, cz) for a in range(3)]
    for c in range(comps):
        cube = gas_ref[c]
        q = cube.reshape(plane, cz)
        x_low = jnp.concatenate([ghost_ref[c, 0:cy], q[: plane - cy]], axis=0)
        x_high = jnp.concatenate([q[cy:], ghost_ref[c, cy : 2 * cy]], axis=0)

        def edge(first):
            ghost = ghost_ref[c, first : first + cx]
            return jnp.broadcast_to(ghost[:, None, :], (cx, cy, cz)).reshape(plane, cz)

        y_low = jnp.where(row_y == 0, edge(2 * cy), pltpu.roll(q, 1, 0))
        y_high = jnp.where(row_y == cy - 1, edge(2 * cy + cx), pltpu.roll(q, plane - 1, 0))
        z_low = jnp.where(lane == 0, z_sides[:, c : c + 1], pltpu.roll(q, 1, 1))
        z_high = jnp.where(lane == cz - 1, z_sides[:, 8 + c : 9 + c], pltpu.roll(q, cz - 1, 1))
        laplace = -6.0 * q + x_high + x_low + y_high + y_low + z_high + z_low
        advect = 0.5 * (
            flow[0] * (x_high - x_low) + flow[1] * (y_high - y_low) + flow[2] * (z_high - z_low)
        )
        own = dep_ref[c, :plane, :] + at_ends(inner, plane, c)
        out_ref[c] = (q + TIME_INCREMENT * (VISCOSITY * laplace - advect + own)).reshape(cx, cy, cz)

    for copy in deposit:
        copy.wait_recv()

    for c in range(comps):
        for side in range(2):
            x_at, y_at = (cx - 1) * side, (cy - 1) * side
            out_ref[c, x_at] += TIME_INCREMENT * dxrecv_ref[side, c]
            out_ref[c, :, y_at, :] += TIME_INCREMENT * dyrecv_ref[side, c]
        for j in range(4):
            dx, dy = DIRS[4 + j]
            x_at, y_at = 0 if dx < 0 else cx - 1, 0 if dy < 0 else cy - 1
            out_ref[c, x_at, y_at : y_at + 1, :] += TIME_INCREMENT * dcrecv_ref[j, c : c + 1, :]

    for copy in halo + z_halo + z_deposit + deposit:
        copy.wait_send()


def local(
    gas_state,
    section_start,
    drop_cell,
    block_tile,
    droplets_per_block,
    drop_frac,
    drop_vel,
    drop_mass,
    drop_temp,
):
    comps, cx, cy, cz = gas_state.shape
    blocks, slots = drop_cell.shape[3:]
    plane = cx * cy
    ghosts = 2 * cx + 2 * cy + 4
    ghost_width = -(-ghosts // LANES) * LANES
    width = plane + ghost_width
    used = plane + -(-ghosts // 16) * 16
    total = blocks * slots
    smem = pl.BlockSpec(memory_space=pltpu.SMEM)
    vmem = pl.BlockSpec(memory_space=pltpu.VMEM)
    section = pl.pallas_call(
        kernel,
        out_shape=jax.ShapeDtypeStruct(gas_state.shape, F32),
        in_specs=[smem] * 2 + [vmem] * 6,
        out_specs=vmem,
        scratch_shapes=[
            pltpu.VMEM((12, blocks, slots), F32),
            pltpu.VMEM((width, total), BF16),
            pltpu.VMEM((cz, total), BF16),
            pltpu.VMEM((blocks, 8, slots), F32),
            pltpu.VMEM((comps * cz, total), BF16),
            pltpu.VMEM((16, total), BF16),
            pltpu.VMEM((comps * cz, width), BF16),
            pltpu.VMEM((comps, ghost_width, cz), F32),
            pltpu.VMEM((2, comps, cx, cz), F32),
            pltpu.VMEM((4, 8, cz), F32),
            pltpu.VMEM((4, 8, cz), F32),
            pltpu.VMEM((2, 8, width), F32),
            pltpu.VMEM((2, 8, width), F32),
            pltpu.VMEM((comps, blocks, slots), F32),
            pltpu.VMEM((comps, blocks, slots), F32),
            pltpu.VMEM((comps, used, cz), F32),
            pltpu.VMEM((4, 8, cz), F32),
            pltpu.VMEM((2, 8, width), F32),
            pltpu.VMEM((2, 8, width), F32),
            pltpu.VMEM((2, comps, cy, cz), F32),
            pltpu.VMEM((2, comps, cx, cz), F32),
            pltpu.VMEM((4, 8, cz), F32),
            pltpu.SemaphoreType.DMA((20,)),
            pltpu.SemaphoreType.DMA((20,)),
        ],
        compiler_params=pltpu.CompilerParams(collective_id=0, has_side_effects=True),
    )(
        block_tile.reshape(block_tile.shape[3:]),
        droplets_per_block.reshape(droplets_per_block.shape[3:]),
        gas_state,
        drop_cell.reshape(drop_cell.shape[3:]),
        drop_frac.reshape(drop_frac.shape[3:]),
        drop_vel.reshape(drop_vel.shape[3:]),
        drop_mass.reshape(drop_mass.shape[3:]),
        drop_temp.reshape(drop_temp.shape[3:]),
    )
    return 0.75 * section_start + 0.25 * section


def solution(mesh):
    in_specs = (
        P(None, "gx", "gy", "gz"),
        P(None, "gx", "gy", "gz"),
        P("gx", "gy", "gz", None, None),
        P("gx", "gy", "gz", None),
        P("gx", "gy", "gz", None),
        P("gx", "gy", "gz", None, None, None),
        P("gx", "gy", "gz", None, None, None),
        P("gx", "gy", "gz", None, None),
        P("gx", "gy", "gz", None, None),
    )
    out_specs = P(None, "gx", "gy", "gz")
    return jax.shard_map(local, mesh=mesh, in_specs=in_specs, out_specs=out_specs, check_vma=False)
```

```python
import functools

import jax
import jax.numpy as jnp
from jax import lax
from jax.experimental import pallas as pl
from jax.experimental.pallas import tpu as pltpu
from jax.sharding import PartitionSpec as P

TS = 8
PARCEL = 8.0
LATENT = 0.5
TIME_INCREMENT = 0.2
VISCOSITY = 0.5
MESH = pl.DeviceIdType.MESH
LANES = 128
F32 = jnp.float32
BF16 = jnp.bfloat16

DIRS = ((-1, 0), (1, 0), (0, -1), (0, 1), (-1, -1), (-1, 1), (1, -1), (1, 1))
OPPOSITE = (1, 0, 3, 2, 7, 6, 5, 4)
DIRS_Z = DIRS + ((0, 0),)
OPPOSITE_Z = OPPOSITE + (8,)


def int_div(values, number):
    if number & (number - 1) == 0:
        return lax.shift_right_logical(values, jnp.int32(number.bit_length() - 1))
    return lax.div(values, jnp.int32(number))


def int_mod(values, number):
    if number & (number - 1) == 0:
        return values & jnp.int32(number - 1)
    return lax.rem(values, jnp.int32(number))


def tap(places, anchor, low, middle, high):
    return jnp.where(
        places == anchor,
        low,
        jnp.where(places == anchor + 1, middle, jnp.where(places == anchor + 2, high, 0.0)),
    )


def kernel(
    tile_in,
    count_in,
    gas_in,
    cell_in,
    frac_in,
    vel_in,
    mass_in,
    temp_in,
    out_ref,
    tile_ref,
    count_ref,
    gas_ref,
    cell_ref,
    frac_ref,
    vel_ref,
    mass_ref,
    temp_ref,
    pick_ref,
    weight_ref,
    planar_ref,
    vert_ref,
    vghost_ref,
    scaled_ref,
    sghost_ref,
    lhs_ref,
    ghost_ref,
    ysend_ref,
    csend_ref,
    crecv_ref,
    zsend_ref,
    zrecv_ref,
    gasat_ref,
    source_ref,
    dep_ref,
    dcsend_ref,
    dzsend_ref,
    dzrecv_ref,
    dxrecv_ref,
    dyrecv_ref,
    dcrecv_ref,
    load_sem,
    send_sem,
    recv_sem,
):
    comps, cx, cy, cz = gas_ref.shape
    blocks, slots = cell_ref.shape
    plane = cx * cy
    starts = (0, cy, 2 * cy, 2 * cy + cx)
    sizes = (cy, cy, cx, cx)
    corner_at = 2 * cy + 2 * cx
    width = planar_ref.shape[0]
    used = plane + dep_ref.shape[1]

    ix, iy, iz = lax.axis_index("gx"), lax.axis_index("gy"), lax.axis_index("gz")
    nx, ny, nz = lax.axis_size("gx"), lax.axis_size("gy"), lax.axis_size("gz")

    def xy_id(k):
        dx, dy = DIRS[k]
        return {"gx": lax.rem(ix + dx + nx, nx), "gy": lax.rem(iy + dy + ny, ny), "gz": iz}

    def z_id(side, j):
        dx, dy = DIRS_Z[j]
        return {
            "gx": lax.rem(ix + dx + nx, nx),
            "gy": lax.rem(iy + dy + ny, ny),
            "gz": lax.rem(iz + (2 * side - 1) + nz, nz),
        }

    pairs = (
        (gas_in, gas_ref),
        (cell_in, cell_ref),
        (frac_in, frac_ref),
        (tile_in, tile_ref),
        (count_in, count_ref),
        (vel_in, vel_ref),
        (mass_in, mass_ref),
        (temp_in, temp_ref),
    )
    loads = [
        pltpu.make_async_copy(src, dst, load_sem.at[i]) for i, (src, dst) in enumerate(pairs)
    ]
    for load in loads:
        load.start()

    barrier = pltpu.get_barrier_semaphore()
    for k in range(8):
        pl.semaphore_signal(barrier, inc=1, device_id=xy_id(k), device_id_type=MESH)
    for side in range(2):
        for j in range(9):
            pl.semaphore_signal(barrier, inc=1, device_id=z_id(side, j), device_id_type=MESH)

    csend_ref[...] = jnp.zeros_like(csend_ref)
    zsend_ref[...] = jnp.zeros_like(zsend_ref)
    ghost_ref[:, corner_at:, :] = jnp.zeros(
        (comps, ghost_ref.shape[1] - corner_at, cz), F32
    )
    for load in loads:
        load.wait()
    ysend_ref[0] = gas_ref[:, :, 0, :]
    ysend_ref[1] = gas_ref[:, :, cy - 1, :]
    for j in range(4):
        dx, dy = DIRS[4 + j]
        csend_ref[j, :comps, :] = gas_ref[:, 0 if dx < 0 else cx - 1, 0 if dy < 0 else cy - 1, :]

    def xy_copy(k, base, src, dst):
        return pltpu.make_async_remote_copy(
            src_ref=src,
            dst_ref=dst,
            send_sem=send_sem.at[base + k],
            recv_sem=recv_sem.at[base + OPPOSITE[k]],
            device_id=xy_id(k),
            device_id_type=MESH,
        )

    cells = cell_ref[...]
    weight_ref[0] = int_div(cells, TS * cz).astype(F32)
    weight_ref[1] = int_mod(int_div(cells, cz), TS).astype(F32)
    weight_ref[2] = int_mod(cells, cz).astype(F32)
    for axis in range(3):
        offset = frac_ref[axis]
        weight_ref[3 + 3 * axis] = 0.5 * (0.5 - offset) * (0.5 - offset)
        weight_ref[4 + 3 * axis] = 0.75 - offset * offset
        weight_ref[5 + 3 * axis] = 0.5 * (0.5 + offset) * (0.5 + offset)

    tiles_y = cy // TS

    def lane_block(b):
        return pl.ds(pl.multiple_of(b * slots, slots), slots)

    def places(rows, first):
        return (lax.broadcasted_iota(jnp.int32, (rows, slots), 0) + first).astype(F32)

    def ends(length):
        row = lax.broadcasted_iota(jnp.int32, (8, slots), 0)
        return jnp.where(row == 0, 0, jnp.where(row == 1, length + 1, -8)).astype(F32)

    def make_weights(b, carry):
        def row(i):
            return weight_ref[i, pl.ds(b, 1), :]

        tile = tile_ref[b]
        corner_x = (int_div(tile, tiles_y) * TS).astype(F32)
        corner_y = (int_mod(tile, tiles_y) * TS).astype(F32)
        anchor_x, anchor_y, anchor_z = row(0) + corner_x, row(1) + corner_y, row(2)
        tx, ty, tz = [tuple(row(3 + 3 * a + i) for i in range(3)) for a in range(3)]
        wx, wxe = tap(places(cx, 1), anchor_x, *tx), tap(ends(cx), anchor_x, *tx)
        wy, wye = tap(places(cy, 1), anchor_y, *ty), tap(ends(cy), anchor_y, *ty)
        corners = [
            wxe[0 if dx < 0 else 1][None] * wye[0 if dy < 0 else 1][None] for dx, dy in DIRS[4:]
        ]
        planar = jnp.concatenate(
            [
                (wx[:, None, :] * wy[None, :, :]).reshape(plane, slots),
                wxe[0:1] * wy,
                wxe[1:2] * wy,
                wx * wye[0:1],
                wx * wye[1:2],
            ]
            + corners
            + [jnp.zeros((width - plane - corner_at - 4, slots), F32)],
            axis=0,
        )
        at = lane_block(b)
        planar_ref[:, at] = planar.astype(BF16)
        vert_ref[:, at] = tap(places(cz, 1), anchor_z, *tz).astype(BF16)
        vghost_ref[b] = tap(ends(cz), anchor_z, *tz).astype(BF16).astype(F32)
        return carry

    lax.fori_loop(0, blocks, make_weights, 0)

    for c in range(comps):
        turned = gas_ref[c].reshape(plane, cz).T
        lhs_ref[c * cz : (c + 1) * cz, :] = turned.astype(BF16)
        zsend_ref[0, c : c + 1, :] = turned[0:1]
        zsend_ref[1, c : c + 1, :] = turned[cz - 1 : cz]

    cell_id = lax.broadcasted_iota(jnp.int32, (plane, LANES), 0)
    ring_id = lax.broadcasted_iota(jnp.int32, (plane, LANES), 1)
    for k in range(8):
        dx, dy = DIRS[k]
        if k < 4:
            step = ring_id - starts[k]
            inside = (step >= 0) & (step < sizes[k])
            if k < 2:
                wanted = step + (cx - 1 if dx < 0 else 0) * cy
            else:
                wanted = step * cy + (cy - 1 if dy < 0 else 0)
        else:
            inside = ring_id == corner_at + k - 4
            wanted = (cx - 1 if dx < 0 else 0) * cy + (cy - 1 if dy < 0 else 0)
        hit = inside & (cell_id == wanted)
        pick_ref[k * plane : (k + 1) * plane, :] = jnp.where(hit, 1.0, 0.0).astype(BF16)

    def z_copies(base, source, dst):
        copies = []
        for j in range(9):
            for side in range(2):
                copies.append(
                    pltpu.make_async_remote_copy(
                        src_ref=source(side, j),
                        dst_ref=dst.at[OPPOSITE_Z[j], 1 - side],
                        send_sem=send_sem.at[base + 2 * j + side],
                        recv_sem=recv_sem.at[base + 2 * OPPOSITE_Z[j] + 1 - side],
                        device_id=z_id(side, j),
                        device_id_type=MESH,
                    )
                )
                copies[-1].start()
        return copies

    pl.semaphore_wait(barrier, 26)

    z_halo = z_copies(8, lambda side, j: zsend_ref.at[side], zrecv_ref)
    halo = []
    for k in (4, 5, 6, 7, 0, 1, 2, 3):
        other = OPPOSITE[k]
        if k < 2:
            src = gas_ref.at[:, 0 if k == 0 else cx - 1]
        elif k < 4:
            src = ysend_ref.at[k - 2]
        else:
            src = csend_ref.at[k - 4]
        if k < 4:
            dst = ghost_ref.at[:, pl.ds(starts[other], sizes[other])]
        else:
            dst = crecv_ref.at[other - 4]
        copy = xy_copy(k, 0, src, dst)
        copy.start()
        halo.append(copy)

    pair = 2 if blocks % 2 == 0 else 1

    def gather(i, carry):
        at = pl.ds(pl.multiple_of(i * pair * slots, pair * slots), pair * slots)
        planar = planar_ref[:plane, at]
        vertical = vert_ref[:, at].astype(F32)
        for c in range(comps):
            near = jnp.dot(
                lhs_ref[c * cz : (c + 1) * cz, :], planar, preferred_element_type=F32
            )
            value = jnp.sum(near * vertical, axis=0, keepdims=True)
            for j in range(pair):
                gasat_ref[c, pl.ds(i * pair + j, 1), :] = value[:, j * slots : (j + 1) * slots]
        return carry

    lax.fori_loop(0, blocks // pair, gather, 0)

    for copy in halo + z_halo:
        copy.wait_recv()

    for c in range(comps):
        ghost_ref[c, corner_at : corner_at + 4, :] = crecv_ref[:, c, :]
    ring = jnp.concatenate(
        [zrecv_ref[j].reshape(16, plane).astype(BF16) for j in range(8)], axis=1
    )
    ring = jnp.dot(ring, pick_ref[...], preferred_element_type=F32)
    z_values = jnp.concatenate([zrecv_ref[8].reshape(16, plane), ring], axis=1).astype(BF16)

    def gather_ghosts(i, carry):
        at = pl.ds(pl.multiple_of(i * pair * slots, pair * slots), pair * slots)
        planar = planar_ref[plane:used, at].astype(F32)
        vertical = vert_ref[:, at]
        near_ends = jnp.dot(z_values, planar_ref[:, at], preferred_element_type=F32)
        low = jnp.concatenate([vghost_ref[i * pair + j, 0:1, :] for j in range(pair)], axis=1)
        high = jnp.concatenate([vghost_ref[i * pair + j, 1:2, :] for j in range(pair)], axis=1)
        both = near_ends[:8] * low + near_ends[8:] * high
        for c in range(comps):
            near = jnp.dot(ghost_ref[c].astype(BF16), vertical, preferred_element_type=F32)
            value = jnp.sum(near * planar, axis=0, keepdims=True) + both[c : c + 1]
            for j in range(pair):
                gasat_ref[c, pl.ds(i * pair + j, 1), :] += value[:, j * slots : (j + 1) * slots]
        return carry

    lax.fori_loop(0, blocks // pair, gather_ghosts, 0)

    temper = temp_ref[...]
    diameter = jnp.exp(jnp.log(mass_ref[...]) * (1.0 / 3.0))
    excess = gasat_ref[4] - temper
    spalding = jnp.maximum(excess, 0.0) + jnp.log1p(jnp.exp(-jnp.abs(excess)))
    rate = diameter * jnp.log1p(spalding)
    drag = diameter * gasat_ref[0]
    heat = diameter * excess
    source_ref[0] = rate
    for a in range(3):
        velocity = vel_ref[a]
        source_ref[1 + a] = rate * velocity - drag * (gasat_ref[1 + a] - velocity)
    source_ref[4] = -heat - LATENT * rate

    sghost_ref[...] = jnp.zeros_like(sghost_ref)
    slot_ids = lax.broadcasted_iota(jnp.int32, (1, slots), 1)

    def scale(b, carry):
        at = lane_block(b)
        alive = jnp.where(slot_ids < count_ref[b], PARCEL, 0.0)
        vertical = vert_ref[:, at].astype(F32)
        low, high = vghost_ref[b, 0:1, :], vghost_ref[b, 1:2, :]
        rows = []
        for c in range(comps):
            strength = source_ref[c, pl.ds(b, 1), :] * alive
            scaled_ref[c * cz : (c + 1) * cz, at] = (vertical * strength).astype(BF16)
            rows.append(strength)
        strengths = jnp.concatenate(rows + [jnp.zeros((8 - comps, slots), F32)], axis=0)
        sghost_ref[:, at] = jnp.concatenate([strengths * low, strengths * high], axis=0).astype(BF16)
        return carry

    lax.fori_loop(0, blocks, scale, 0)

    def contract(lhs, rhs):
        return lax.dot_general(lhs, rhs, (((1,), (1,)), ((), ())), preferred_element_type=F32)

    z_ends = contract(sghost_ref[...], planar_ref[...])
    for side in range(2):
        dzsend_ref[0, side] = z_ends[8 * side : 8 * side + 8, :plane]
        dzsend_ref[1, side] = z_ends[8 * side : 8 * side + 8, plane:]
    z_deposit = z_copies(34, lambda side, j: dzsend_ref.at[0 if j == 8 else 1, side], dzrecv_ref)

    dcsend_ref[...] = jnp.zeros_like(dcsend_ref)
    for c in range(comps):
        ghosts = contract(planar_ref[plane:used, :], scaled_ref[c * cz : (c + 1) * cz, :])
        dep_ref[c] = ghosts
        for j in range(4):
            dcsend_ref[j, c : c + 1, :] = ghosts[corner_at + j : corner_at + j + 1]

    deposit = []
    for k in (4, 5, 6, 7, 0, 1, 2, 3):
        other = OPPOSITE[k]
        if k < 4:
            src = dep_ref.at[:, pl.ds(starts[k], sizes[k])]
            dst = (dxrecv_ref if k < 2 else dyrecv_ref).at[other % 2]
        else:
            src, dst = dcsend_ref.at[k - 4], dcrecv_ref.at[other - 4]
        copy = xy_copy(k, 26, src, dst)
        copy.start()
        deposit.append(copy)

    lane = lax.broadcasted_iota(jnp.int32, (plane, cz), 1)
    row_y = int_mod(lax.broadcasted_iota(jnp.int32, (plane, cz), 0), cy)

    def columns(ref):
        both = ref[8].reshape(16, plane)
        return jnp.concatenate([both, jnp.zeros((LANES - 16, plane), F32)], axis=0).T

    def at_ends(turned, first, rows, at):
        lanes = lax.broadcasted_iota(jnp.int32, (rows, cz), 1)
        low = turned[first : first + rows, at : at + 1]
        high = turned[first : first + rows, 8 + at : 9 + at]
        return jnp.where(lanes == 0, low, 0.0) + jnp.where(lanes == cz - 1, high, 0.0)

    z_sides = columns(zrecv_ref)
    flow = [gas_ref[1 + a].reshape(plane, cz) for a in range(3)]
    for c in range(comps):
        cube = gas_ref[c]
        q = cube.reshape(plane, cz)
        x_low = jnp.concatenate([ghost_ref[c, 0:cy], q[: plane - cy]], axis=0)
        x_high = jnp.concatenate([q[cy:], ghost_ref[c, cy : 2 * cy]], axis=0)

        def edge(first):
            ghost = ghost_ref[c, first : first + cx]
            return jnp.broadcast_to(ghost[:, None, :], (cx, cy, cz)).reshape(plane, cz)

        y_low = jnp.where(row_y == 0, edge(2 * cy), pltpu.roll(q, 1, 0))
        y_high = jnp.where(row_y == cy - 1, edge(2 * cy + cx), pltpu.roll(q, plane - 1, 0))
        z_low = jnp.where(lane == 0, z_sides[:, c : c + 1], pltpu.roll(q, 1, 1))
        z_high = jnp.where(lane == cz - 1, z_sides[:, 8 + c : 9 + c], pltpu.roll(q, cz - 1, 1))
        laplace = -6.0 * q + x_high + x_low + y_high + y_low + z_high + z_low
        advect = 0.5 * (
            flow[0] * (x_high - x_low) + flow[1] * (y_high - y_low) + flow[2] * (z_high - z_low)
        )
        own = contract(planar_ref[:plane, :], scaled_ref[c * cz : (c + 1) * cz, :])
        out_ref[c] = (q + TIME_INCREMENT * (VISCOSITY * laplace - advect + own)).reshape(cx, cy, cz)

    for copy in z_deposit + deposit:
        copy.wait_recv()

    inner = columns(dzrecv_ref)
    outer = jnp.concatenate([dzrecv_ref[j].reshape(16, LANES) for j in range(8)], axis=0).T
    for c in range(comps):
        ends_c = at_ends(inner, 0, plane, c)
        out_ref[c] += TIME_INCREMENT * ends_c.reshape(cx, cy, cz)
        for side in range(2):
            x_at, y_at = (cx - 1) * side, (cy - 1) * side
            x_ends = at_ends(outer, starts[1 - side], cy, 16 * side + c)
            y_ends = at_ends(outer, starts[3 - side], cx, 16 * (2 + side) + c)
            out_ref[c, x_at] += TIME_INCREMENT * (dxrecv_ref[side, c] + x_ends)
            out_ref[c, :, y_at, :] += TIME_INCREMENT * (dyrecv_ref[side, c] + y_ends)
        for j in range(4):
            dx, dy = DIRS[4 + j]
            x_at, y_at = 0 if dx < 0 else cx - 1, 0 if dy < 0 else cy - 1
            corner = at_ends(outer, corner_at + OPPOSITE[4 + j] - 4, 1, 16 * (4 + j) + c)
            out_ref[c, x_at, y_at : y_at + 1, :] += TIME_INCREMENT * (
                dcrecv_ref[j, c : c + 1, :] + corner
            )

    for copy in halo + z_halo + z_deposit + deposit:
        copy.wait_send()


def local(
    gas_state,
    section_start,
    drop_cell,
    block_tile,
    droplets_per_block,
    drop_frac,
    drop_vel,
    drop_mass,
    drop_temp,
):
    comps, cx, cy, cz = gas_state.shape
    blocks, slots = drop_cell.shape[3:]
    plane = cx * cy
    ghosts = 2 * cx + 2 * cy + 4
    ghost_width = -(-ghosts // LANES) * LANES
    width = plane + ghost_width
    used = plane + -(-ghosts // 16) * 16
    total = blocks * slots
    vmem = pl.BlockSpec(memory_space=pltpu.VMEM)
    section = pl.pallas_call(
        kernel,
        out_shape=jax.ShapeDtypeStruct(gas_state.shape, F32),
        in_specs=[pl.BlockSpec(memory_space=pl.ANY)] * 8,
        out_specs=vmem,
        scratch_shapes=[
            pltpu.SMEM((blocks,), jnp.int32),
            pltpu.SMEM((blocks,), jnp.int32),
            pltpu.VMEM(gas_state.shape, F32),
            pltpu.VMEM((blocks, slots), jnp.int32),
            pltpu.VMEM((3, blocks, slots), F32),
            pltpu.VMEM((3, blocks, slots), F32),
            pltpu.VMEM((blocks, slots), F32),
            pltpu.VMEM((blocks, slots), F32),
            pltpu.VMEM((8 * plane, ghost_width), BF16),
            pltpu.VMEM((12, blocks, slots), F32),
            pltpu.VMEM((width, total), BF16),
            pltpu.VMEM((cz, total), BF16),
            pltpu.VMEM((blocks, 8, slots), F32),
            pltpu.VMEM((comps * cz, total), BF16),
            pltpu.VMEM((16, total), BF16),
            pltpu.VMEM((comps * cz, plane), BF16),
            pltpu.VMEM((comps, used - plane, cz), F32),
            pltpu.VMEM((2, comps, cx, cz), F32),
            pltpu.VMEM((4, 8, cz), F32),
            pltpu.VMEM((4, 8, cz), F32),
            pltpu.VMEM((2, 8, plane), F32),
            pltpu.VMEM((9, 2, 8, plane), F32),
            pltpu.VMEM((comps, blocks, slots), F32),
            pltpu.VMEM((comps, blocks, slots), F32),
            pltpu.VMEM((comps, used - plane, cz), F32),
            pltpu.VMEM((4, 8, cz), F32),
            pltpu.VMEM((2, 2, 8, ghost_width), F32),
            pltpu.VMEM((9, 2, 8, ghost_width), F32),
            pltpu.VMEM((2, comps, cy, cz), F32),
            pltpu.VMEM((2, comps, cx, cz), F32),
            pltpu.VMEM((4, 8, cz), F32),
            pltpu.SemaphoreType.DMA((8,)),
            pltpu.SemaphoreType.DMA((52,)),
            pltpu.SemaphoreType.DMA((52,)),
        ],
        compiler_params=pltpu.CompilerParams(collective_id=0, has_side_effects=True),
    )(
        block_tile.reshape(block_tile.shape[3:]),
        droplets_per_block.reshape(droplets_per_block.shape[3:]),
        gas_state,
        drop_cell.reshape(drop_cell.shape[3:]),
        drop_frac.reshape(drop_frac.shape[3:]),
        drop_vel.reshape(drop_vel.shape[3:]),
        drop_mass.reshape(drop_mass.shape[3:]),
        drop_temp.reshape(drop_temp.shape[3:]),
    )
    return 0.75 * section_start + 0.25 * section


def solution(mesh):
    in_specs = (
        P(None, "gx", "gy", "gz"),
        P(None, "gx", "gy", "gz"),
        P("gx", "gy", "gz", None, None),
        P("gx", "gy", "gz", None),
        P("gx", "gy", "gz", None),
        P("gx", "gy", "gz", None, None, None),
        P("gx", "gy", "gz", None, None, None),
        P("gx", "gy", "gz", None, None),
        P("gx", "gy", "gz", None, None),
    )
    out_specs = P(None, "gx", "gy", "gz")
    return jax.shard_map(local, mesh=mesh, in_specs=in_specs, out_specs=out_specs, check_vma=False)
```

```python
import functools

import jax
import jax.numpy as jnp
from jax import lax
from jax.experimental import pallas as pl
from jax.experimental.pallas import tpu as pltpu
from jax.sharding import PartitionSpec as P

TS = 8
PARCEL = 8.0
LATENT = 0.5
TIME_INCREMENT = 0.2
VISCOSITY = 0.5
MESH = pl.DeviceIdType.MESH
LANES = 128
F32 = jnp.float32
BF16 = jnp.bfloat16

DIRS = ((-1, 0), (1, 0), (0, -1), (0, 1), (-1, -1), (-1, 1), (1, -1), (1, 1))
OPPOSITE = (1, 0, 3, 2, 7, 6, 5, 4)
DIRS_Z = DIRS + ((0, 0),)
OPPOSITE_Z = OPPOSITE + (8,)


def int_div(values, number):
    if number & (number - 1) == 0:
        return lax.shift_right_logical(values, jnp.int32(number.bit_length() - 1))
    return lax.div(values, jnp.int32(number))


def int_mod(values, number):
    if number & (number - 1) == 0:
        return values & jnp.int32(number - 1)
    return lax.rem(values, jnp.int32(number))


def tap(places, anchor, low, middle, high):
    return jnp.where(
        places == anchor,
        low,
        jnp.where(places == anchor + 1, middle, jnp.where(places == anchor + 2, high, 0.0)),
    )


def kernel(
    tile_in,
    count_in,
    gas_in,
    cell_in,
    frac_in,
    vel_in,
    mass_in,
    temp_in,
    out_ref,
    tile_ref,
    count_ref,
    gas_ref,
    cell_ref,
    frac_ref,
    vel_ref,
    mass_ref,
    temp_ref,
    pick_ref,
    weight_ref,
    planar_ref,
    vert_ref,
    vghost_ref,
    scaled_ref,
    sghost_ref,
    lhs_ref,
    ghost_ref,
    ysend_ref,
    csend_ref,
    crecv_ref,
    zsend_ref,
    zrecv_ref,
    gasat_ref,
    source_ref,
    dep_ref,
    dcsend_ref,
    dzsend_ref,
    dzrecv_ref,
    dxrecv_ref,
    dyrecv_ref,
    dcrecv_ref,
    load_sem,
    send_sem,
    recv_sem,
):
    comps, cx, cy, cz = gas_ref.shape
    blocks, slots = cell_ref.shape
    plane = cx * cy
    starts = (0, cy, 2 * cy, 2 * cy + cx)
    sizes = (cy, cy, cx, cx)
    corner_at = 2 * cy + 2 * cx
    width = planar_ref.shape[0]
    used = plane + dep_ref.shape[1]

    ix, iy, iz = lax.axis_index("gx"), lax.axis_index("gy"), lax.axis_index("gz")
    nx, ny, nz = lax.axis_size("gx"), lax.axis_size("gy"), lax.axis_size("gz")

    def xy_id(k):
        dx, dy = DIRS[k]
        return {"gx": lax.rem(ix + dx + nx, nx), "gy": lax.rem(iy + dy + ny, ny), "gz": iz}

    def z_id(side, j):
        dx, dy = DIRS_Z[j]
        return {
            "gx": lax.rem(ix + dx + nx, nx),
            "gy": lax.rem(iy + dy + ny, ny),
            "gz": lax.rem(iz + (2 * side - 1) + nz, nz),
        }

    pairs = (
        (gas_in, gas_ref),
        (cell_in, cell_ref),
        (frac_in, frac_ref),
        (tile_in, tile_ref),
        (count_in, count_ref),
        (vel_in, vel_ref),
        (mass_in, mass_ref),
        (temp_in, temp_ref),
    )
    loads = [
        pltpu.make_async_copy(src, dst, load_sem.at[i]) for i, (src, dst) in enumerate(pairs)
    ]
    for load in loads:
        load.start()

    barrier = pltpu.get_barrier_semaphore()
    for k in range(8):
        pl.semaphore_signal(barrier, inc=1, device_id=xy_id(k), device_id_type=MESH)
    z_sides_apart = range(2) if nz > 2 else range(1)
    for side in z_sides_apart:
        for j in range(9):
            pl.semaphore_signal(barrier, inc=1, device_id=z_id(side, j), device_id_type=MESH)

    csend_ref[...] = jnp.zeros_like(csend_ref)
    zsend_ref[...] = jnp.zeros_like(zsend_ref)
    ghost_ref[:, corner_at:, :] = jnp.zeros(
        (comps, ghost_ref.shape[1] - corner_at, cz), F32
    )
    loads[0].wait()
    ysend_ref[0] = gas_ref[:, :, 0, :]
    ysend_ref[1] = gas_ref[:, :, cy - 1, :]
    for j in range(4):
        dx, dy = DIRS[4 + j]
        csend_ref[j, :comps, :] = gas_ref[:, 0 if dx < 0 else cx - 1, 0 if dy < 0 else cy - 1, :]

    def xy_copy(k, base, src, dst):
        return pltpu.make_async_remote_copy(
            src_ref=src,
            dst_ref=dst,
            send_sem=send_sem.at[base + k],
            recv_sem=recv_sem.at[base + OPPOSITE[k]],
            device_id=xy_id(k),
            device_id_type=MESH,
        )

    for c in range(comps):
        turned = gas_ref[c].reshape(plane, cz).T
        lhs_ref[c * cz : (c + 1) * cz, :] = turned.astype(BF16)
        zsend_ref[1, c : c + 1, :] = turned[0:1]
        zsend_ref[0, c : c + 1, :] = turned[cz - 1 : cz]

    def z_copies(base, source, dst):
        copies = []
        for j in range(9):
            for side in z_sides_apart:
                src, at = source(j), OPPOSITE_Z[j]
                apart = len(z_sides_apart) == 2
                copies.append(
                    pltpu.make_async_remote_copy(
                        src_ref=src.at[1 - side] if apart else src,
                        dst_ref=dst.at[at, 1 - side] if apart else dst.at[at],
                        send_sem=send_sem.at[base + 2 * j + side],
                        recv_sem=recv_sem.at[base + 2 * at + (1 - side if apart else 0)],
                        device_id=z_id(side, j),
                        device_id_type=MESH,
                    )
                )
                copies[-1].start()
        return copies

    pl.semaphore_wait(barrier, 8 + 9 * len(z_sides_apart))

    z_halo = z_copies(8, lambda j: zsend_ref, zrecv_ref)
    halo = []
    for k in (4, 5, 6, 7, 0, 1, 2, 3):
        other = OPPOSITE[k]
        if k < 2:
            src = gas_ref.at[:, 0 if k == 0 else cx - 1]
        elif k < 4:
            src = ysend_ref.at[k - 2]
        else:
            src = csend_ref.at[k - 4]
        if k < 4:
            dst = ghost_ref.at[:, pl.ds(starts[other], sizes[other])]
        else:
            dst = crecv_ref.at[other - 4]
        copy = xy_copy(k, 0, src, dst)
        copy.start()
        halo.append(copy)

    for load in loads[1:]:
        load.wait()
    cells = cell_ref[...]
    weight_ref[0] = int_div(cells, TS * cz).astype(F32)
    weight_ref[1] = int_mod(int_div(cells, cz), TS).astype(F32)
    weight_ref[2] = int_mod(cells, cz).astype(F32)
    for axis in range(3):
        offset = frac_ref[axis]
        weight_ref[3 + 3 * axis] = 0.5 * (0.5 - offset) * (0.5 - offset)
        weight_ref[4 + 3 * axis] = 0.75 - offset * offset
        weight_ref[5 + 3 * axis] = 0.5 * (0.5 + offset) * (0.5 + offset)

    tiles_y = cy // TS

    def lane_block(b):
        return pl.ds(pl.multiple_of(b * slots, slots), slots)

    def places(rows, first):
        return (lax.broadcasted_iota(jnp.int32, (rows, slots), 0) + first).astype(F32)

    def ends(length):
        row = lax.broadcasted_iota(jnp.int32, (8, slots), 0)
        return jnp.where(row == 0, 0, jnp.where(row == 1, length + 1, -8)).astype(F32)

    def make_weights(b, carry):
        def row(i):
            return weight_ref[i, pl.ds(b, 1), :]

        tile = tile_ref[b]
        corner_x = (int_div(tile, tiles_y) * TS).astype(F32)
        corner_y = (int_mod(tile, tiles_y) * TS).astype(F32)
        anchor_x, anchor_y, anchor_z = row(0) + corner_x, row(1) + corner_y, row(2)
        tx, ty, tz = [tuple(row(3 + 3 * a + i) for i in range(3)) for a in range(3)]
        wx, wxe = tap(places(cx, 1), anchor_x, *tx), tap(ends(cx), anchor_x, *tx)
        wy, wye = tap(places(cy, 1), anchor_y, *ty), tap(ends(cy), anchor_y, *ty)
        corners = [
            wxe[0 if dx < 0 else 1][None] * wye[0 if dy < 0 else 1][None] for dx, dy in DIRS[4:]
        ]
        planar = jnp.concatenate(
            [
                (wx[:, None, :] * wy[None, :, :]).reshape(plane, slots),
                wxe[0:1] * wy,
                wxe[1:2] * wy,
                wx * wye[0:1],
                wx * wye[1:2],
            ]
            + corners
            + [jnp.zeros((width - plane - corner_at - 4, slots), F32)],
            axis=0,
        )
        at = lane_block(b)
        planar_ref[:, at] = planar.astype(BF16)
        vert_ref[:, at] = tap(places(cz, 1), anchor_z, *tz).astype(BF16)
        vghost_ref[b] = tap(ends(cz), anchor_z, *tz).astype(BF16).astype(F32)
        return carry

    lax.fori_loop(0, blocks, make_weights, 0)

    cell_id = lax.broadcasted_iota(jnp.int32, (plane, LANES), 0)
    ring_id = lax.broadcasted_iota(jnp.int32, (plane, LANES), 1)
    for k in range(8):
        dx, dy = DIRS[k]
        if k < 4:
            step = ring_id - starts[k]
            inside = (step >= 0) & (step < sizes[k])
            if k < 2:
                wanted = step + (cx - 1 if dx < 0 else 0) * cy
            else:
                wanted = step * cy + (cy - 1 if dy < 0 else 0)
        else:
            inside = ring_id == corner_at + k - 4
            wanted = (cx - 1 if dx < 0 else 0) * cy + (cy - 1 if dy < 0 else 0)
        hit = inside & (cell_id == wanted)
        pick_ref[k * plane : (k + 1) * plane, :] = jnp.where(hit, 1.0, 0.0).astype(BF16)

    pair = 2 if blocks % 2 == 0 else 1

    def gather(i, carry):
        at = pl.ds(pl.multiple_of(i * pair * slots, pair * slots), pair * slots)
        planar = planar_ref[:plane, at]
        vertical = vert_ref[:, at].astype(F32)
        near = jnp.dot(lhs_ref[...], planar, preferred_element_type=F32)
        for c in range(comps):
            value = jnp.sum(near[c * cz : (c + 1) * cz] * vertical, axis=0, keepdims=True)
            for j in range(pair):
                gasat_ref[c, pl.ds(i * pair + j, 1), :] = value[:, j * slots : (j + 1) * slots]
        return carry

    lax.fori_loop(0, blocks // pair, gather, 0)

    for copy in halo + z_halo:
        copy.wait_recv()

    for c in range(comps):
        ghost_ref[c, corner_at : corner_at + 4, :] = crecv_ref[:, c, :]
    ring = jnp.concatenate(
        [zrecv_ref[j].reshape(16, plane).astype(BF16) for j in range(8)], axis=1
    )
    ring = jnp.dot(ring, pick_ref[...], preferred_element_type=F32)
    z_values = jnp.concatenate([zrecv_ref[8].reshape(16, plane), ring], axis=1).astype(BF16)

    ghost_rows = ghost_ref[...].reshape(comps * (used - plane), cz).astype(BF16)

    def gather_ghosts(i, carry):
        at = pl.ds(pl.multiple_of(i * pair * slots, pair * slots), pair * slots)
        planar = planar_ref[plane:used, at].astype(F32)
        vertical = vert_ref[:, at]
        near_ends = jnp.dot(z_values, planar_ref[:, at], preferred_element_type=F32)
        low = jnp.concatenate([vghost_ref[i * pair + j, 0:1, :] for j in range(pair)], axis=1)
        high = jnp.concatenate([vghost_ref[i * pair + j, 1:2, :] for j in range(pair)], axis=1)
        both = near_ends[:8] * low + near_ends[8:] * high
        near = jnp.dot(ghost_rows, vertical, preferred_element_type=F32)
        for c in range(comps):
            part = near[c * (used - plane) : (c + 1) * (used - plane)]
            value = jnp.sum(part * planar, axis=0, keepdims=True) + both[c : c + 1]
            for j in range(pair):
                gasat_ref[c, pl.ds(i * pair + j, 1), :] += value[:, j * slots : (j + 1) * slots]
        return carry

    lax.fori_loop(0, blocks // pair, gather_ghosts, 0)

    temper = temp_ref[...]
    diameter = jnp.exp(jnp.log(mass_ref[...]) * (1.0 / 3.0))
    excess = gasat_ref[4] - temper
    spalding = jnp.maximum(excess, 0.0) + jnp.log1p(jnp.exp(-jnp.abs(excess)))
    rate = diameter * jnp.log1p(spalding)
    drag = diameter * gasat_ref[0]
    heat = diameter * excess
    source_ref[0] = rate
    for a in range(3):
        velocity = vel_ref[a]
        source_ref[1 + a] = rate * velocity - drag * (gasat_ref[1 + a] - velocity)
    source_ref[4] = -heat - LATENT * rate

    sghost_ref[...] = jnp.zeros_like(sghost_ref)
    slot_ids = lax.broadcasted_iota(jnp.int32, (1, slots), 1)

    def scale(b, carry):
        at = lane_block(b)
        alive = jnp.where(slot_ids < count_ref[b], PARCEL, 0.0)
        vertical = vert_ref[:, at].astype(F32)
        low, high = vghost_ref[b, 0:1, :], vghost_ref[b, 1:2, :]
        rows = []
        for c in range(comps):
            strength = source_ref[c, pl.ds(b, 1), :] * alive
            scaled_ref[c * cz : (c + 1) * cz, at] = (vertical * strength).astype(BF16)
            rows.append(strength)
        strengths = jnp.concatenate(rows + [jnp.zeros((8 - comps, slots), F32)], axis=0)
        sghost_ref[:, at] = jnp.concatenate([strengths * low, strengths * high], axis=0).astype(BF16)
        return carry

    lax.fori_loop(0, blocks, scale, 0)

    def contract(lhs, rhs):
        return lax.dot_general(lhs, rhs, (((1,), (1,)), ((), ())), preferred_element_type=F32)

    z_ends = contract(sghost_ref[...], planar_ref[...])
    for side in range(2):
        dzsend_ref[0, 1 - side] = z_ends[8 * side : 8 * side + 8, :plane]
        dzsend_ref[1, 1 - side] = z_ends[8 * side : 8 * side + 8, plane:]
    z_deposit = z_copies(34, lambda j: dzsend_ref.at[0 if j == 8 else 1], dzrecv_ref)

    dcsend_ref[...] = jnp.zeros_like(dcsend_ref)
    all_ghosts = contract(planar_ref[plane:used, :], scaled_ref[...])
    for c in range(comps):
        ghosts = all_ghosts[:, c * cz : (c + 1) * cz]
        dep_ref[c] = ghosts
        for j in range(4):
            dcsend_ref[j, c : c + 1, :] = ghosts[corner_at + j : corner_at + j + 1]

    deposit = []
    for k in (4, 5, 6, 7, 0, 1, 2, 3):
        other = OPPOSITE[k]
        if k < 4:
            src = dep_ref.at[:, pl.ds(starts[k], sizes[k])]
            dst = (dxrecv_ref if k < 2 else dyrecv_ref).at[other % 2]
        else:
            src, dst = dcsend_ref.at[k - 4], dcrecv_ref.at[other - 4]
        copy = xy_copy(k, 26, src, dst)
        copy.start()
        deposit.append(copy)

    lane = lax.broadcasted_iota(jnp.int32, (plane, cz), 1)
    row_y = int_mod(lax.broadcasted_iota(jnp.int32, (plane, cz), 0), cy)

    def columns(ref):
        both = ref[8].reshape(16, plane)
        return jnp.concatenate([both, jnp.zeros((LANES - 16, plane), F32)], axis=0).T

    def at_ends(turned, first, rows, at):
        lanes = lax.broadcasted_iota(jnp.int32, (rows, cz), 1)
        low = turned[first : first + rows, at : at + 1]
        high = turned[first : first + rows, 8 + at : 9 + at]
        return jnp.where(lanes == 0, low, 0.0) + jnp.where(lanes == cz - 1, high, 0.0)

    z_sides = columns(zrecv_ref)
    all_own = contract(planar_ref[:plane, :], scaled_ref[...])
    flow = [gas_ref[1 + a].reshape(plane, cz) for a in range(3)]
    for c in range(comps):
        cube = gas_ref[c]
        q = cube.reshape(plane, cz)
        x_low = jnp.concatenate([ghost_ref[c, 0:cy], q[: plane - cy]], axis=0)
        x_high = jnp.concatenate([q[cy:], ghost_ref[c, cy : 2 * cy]], axis=0)

        def edge(first):
            ghost = ghost_ref[c, first : first + cx]
            return jnp.broadcast_to(ghost[:, None, :], (cx, cy, cz)).reshape(plane, cz)

        y_low = jnp.where(row_y == 0, edge(2 * cy), pltpu.roll(q, 1, 0))
        y_high = jnp.where(row_y == cy - 1, edge(2 * cy + cx), pltpu.roll(q, plane - 1, 0))
        z_low = jnp.where(lane == 0, z_sides[:, c : c + 1], pltpu.roll(q, 1, 1))
        z_high = jnp.where(lane == cz - 1, z_sides[:, 8 + c : 9 + c], pltpu.roll(q, cz - 1, 1))
        laplace = -6.0 * q + x_high + x_low + y_high + y_low + z_high + z_low
        advect = 0.5 * (
            flow[0] * (x_high - x_low) + flow[1] * (y_high - y_low) + flow[2] * (z_high - z_low)
        )
        own = all_own[:, c * cz : (c + 1) * cz]
        out_ref[c] = (q + TIME_INCREMENT * (VISCOSITY * laplace - advect + own)).reshape(cx, cy, cz)

    for copy in z_deposit + deposit:
        copy.wait_recv()

    inner = columns(dzrecv_ref)
    outer = jnp.concatenate([dzrecv_ref[j].reshape(16, LANES) for j in range(8)], axis=0).T
    for c in range(comps):
        ends_c = at_ends(inner, 0, plane, c)
        out_ref[c] += TIME_INCREMENT * ends_c.reshape(cx, cy, cz)
        for side in range(2):
            x_at, y_at = (cx - 1) * side, (cy - 1) * side
            x_ends = at_ends(outer, starts[1 - side], cy, 16 * side + c)
            y_ends = at_ends(outer, starts[3 - side], cx, 16 * (2 + side) + c)
            out_ref[c, x_at] += TIME_INCREMENT * (dxrecv_ref[side, c] + x_ends)
            out_ref[c, :, y_at, :] += TIME_INCREMENT * (dyrecv_ref[side, c] + y_ends)
        for j in range(4):
            dx, dy = DIRS[4 + j]
            x_at, y_at = 0 if dx < 0 else cx - 1, 0 if dy < 0 else cy - 1
            corner = at_ends(outer, corner_at + OPPOSITE[4 + j] - 4, 1, 16 * (4 + j) + c)
            out_ref[c, x_at, y_at : y_at + 1, :] += TIME_INCREMENT * (
                dcrecv_ref[j, c : c + 1, :] + corner
            )

    for copy in halo + z_halo + z_deposit + deposit:
        copy.wait_send()


def local(
    gas_state,
    section_start,
    drop_cell,
    block_tile,
    droplets_per_block,
    drop_frac,
    drop_vel,
    drop_mass,
    drop_temp,
):
    comps, cx, cy, cz = gas_state.shape
    blocks, slots = drop_cell.shape[3:]
    plane = cx * cy
    ghosts = 2 * cx + 2 * cy + 4
    ghost_width = -(-ghosts // LANES) * LANES
    width = plane + ghost_width
    used = plane + -(-ghosts // 16) * 16
    total = blocks * slots
    vmem = pl.BlockSpec(memory_space=pltpu.VMEM)
    section = pl.pallas_call(
        kernel,
        out_shape=pltpu.VMEM(gas_state.shape, F32),
        in_specs=[pl.BlockSpec(memory_space=pl.ANY)] * 8,
        out_specs=vmem,
        scratch_shapes=[
            pltpu.SMEM((blocks,), jnp.int32),
            pltpu.SMEM((blocks,), jnp.int32),
            pltpu.VMEM(gas_state.shape, F32),
            pltpu.VMEM((blocks, slots), jnp.int32),
            pltpu.VMEM((3, blocks, slots), F32),
            pltpu.VMEM((3, blocks, slots), F32),
            pltpu.VMEM((blocks, slots), F32),
            pltpu.VMEM((blocks, slots), F32),
            pltpu.VMEM((8 * plane, ghost_width), BF16),
            pltpu.VMEM((12, blocks, slots), F32),
            pltpu.VMEM((width, total), BF16),
            pltpu.VMEM((cz, total), BF16),
            pltpu.VMEM((blocks, 8, slots), F32),
            pltpu.VMEM((comps * cz, total), BF16),
            pltpu.VMEM((16, total), BF16),
            pltpu.VMEM((comps * cz, plane), BF16),
            pltpu.VMEM((comps, used - plane, cz), F32),
            pltpu.VMEM((2, comps, cx, cz), F32),
            pltpu.VMEM((4, 8, cz), F32),
            pltpu.VMEM((4, 8, cz), F32),
            pltpu.VMEM((2, 8, plane), F32),
            pltpu.VMEM((9, 2, 8, plane), F32),
            pltpu.VMEM((comps, blocks, slots), F32),
            pltpu.VMEM((comps, blocks, slots), F32),
            pltpu.VMEM((comps, used - plane, cz), F32),
            pltpu.VMEM((4, 8, cz), F32),
            pltpu.VMEM((2, 2, 8, ghost_width), F32),
            pltpu.VMEM((9, 2, 8, ghost_width), F32),
            pltpu.VMEM((2, comps, cy, cz), F32),
            pltpu.VMEM((2, comps, cx, cz), F32),
            pltpu.VMEM((4, 8, cz), F32),
            pltpu.SemaphoreType.DMA((8,)),
            pltpu.SemaphoreType.DMA((52,)),
            pltpu.SemaphoreType.DMA((52,)),
        ],
        compiler_params=pltpu.CompilerParams(collective_id=0, has_side_effects=True),
    )(
        block_tile.reshape(block_tile.shape[3:]),
        droplets_per_block.reshape(droplets_per_block.shape[3:]),
        gas_state,
        drop_cell.reshape(drop_cell.shape[3:]),
        drop_frac.reshape(drop_frac.shape[3:]),
        drop_vel.reshape(drop_vel.shape[3:]),
        drop_mass.reshape(drop_mass.shape[3:]),
        drop_temp.reshape(drop_temp.shape[3:]),
    )
    return 0.75 * section_start + 0.25 * section


def solution(mesh):
    in_specs = (
        P(None, "gx", "gy", "gz"),
        P(None, "gx", "gy", "gz"),
        P("gx", "gy", "gz", None, None),
        P("gx", "gy", "gz", None),
        P("gx", "gy", "gz", None),
        P("gx", "gy", "gz", None, None, None),
        P("gx", "gy", "gz", None, None, None),
        P("gx", "gy", "gz", None, None),
        P("gx", "gy", "gz", None, None),
    )
    out_specs = P(None, "gx", "gy", "gz")
    return jax.shard_map(local, mesh=mesh, in_specs=in_specs, out_specs=out_specs, check_vma=False)
```

```python
import functools

import jax
import jax.numpy as jnp
from jax import lax
from jax.experimental import pallas as pl
from jax.experimental.pallas import tpu as pltpu
from jax.sharding import PartitionSpec as P

TS = 8
PARCEL = 8.0
LATENT = 0.5
TIME_INCREMENT = 0.2
VISCOSITY = 0.5
MESH = pl.DeviceIdType.MESH
LANES = 128
F32 = jnp.float32
BF16 = jnp.bfloat16

DIRS = ((-1, 0), (1, 0), (0, -1), (0, 1), (-1, -1), (-1, 1), (1, -1), (1, 1))
OPPOSITE = (1, 0, 3, 2, 7, 6, 5, 4)
DIRS_Z = DIRS + ((0, 0),)
OPPOSITE_Z = OPPOSITE + (8,)


def int_div(values, number):
    if number & (number - 1) == 0:
        return lax.shift_right_logical(values, jnp.int32(number.bit_length() - 1))
    return lax.div(values, jnp.int32(number))


def int_mod(values, number):
    if number & (number - 1) == 0:
        return values & jnp.int32(number - 1)
    return lax.rem(values, jnp.int32(number))


def tap(places, anchor, low, middle, high):
    return jnp.where(
        places == anchor,
        low,
        jnp.where(places == anchor + 1, middle, jnp.where(places == anchor + 2, high, 0.0)),
    )


def kernel(
    tile_in,
    count_in,
    gas_in,
    cell_in,
    frac_in,
    vel_in,
    mass_in,
    temp_in,
    out_ref,
    tile_ref,
    count_ref,
    gas_ref,
    cell_ref,
    frac_ref,
    vel_ref,
    mass_ref,
    temp_ref,
    pick_ref,
    weight_ref,
    planar_ref,
    vert_ref,
    vghost_ref,
    scaled_ref,
    sghost_ref,
    lhs_ref,
    ghost_ref,
    ysend_ref,
    csend_ref,
    crecv_ref,
    zsend_ref,
    zrecv_ref,
    gasat_ref,
    source_ref,
    dep_ref,
    dcsend_ref,
    dzsend_ref,
    dzrecv_ref,
    dxrecv_ref,
    dyrecv_ref,
    dcrecv_ref,
    load_sem,
    send_sem,
    recv_sem,
):
    comps, cx, cy, cz = gas_ref.shape
    blocks, slots = cell_ref.shape
    plane = cx * cy
    starts = (0, cy, 2 * cy, 2 * cy + cx)
    sizes = (cy, cy, cx, cx)
    corner_at = 2 * cy + 2 * cx
    width = planar_ref.shape[0]
    used = plane + dep_ref.shape[1]

    ix, iy, iz = lax.axis_index("gx"), lax.axis_index("gy"), lax.axis_index("gz")
    nx, ny, nz = lax.axis_size("gx"), lax.axis_size("gy"), lax.axis_size("gz")

    def xy_id(k):
        dx, dy = DIRS[k]
        return {"gx": lax.rem(ix + dx + nx, nx), "gy": lax.rem(iy + dy + ny, ny), "gz": iz}

    def z_id(side, j):
        dx, dy = DIRS_Z[j]
        return {
            "gx": lax.rem(ix + dx + nx, nx),
            "gy": lax.rem(iy + dy + ny, ny),
            "gz": lax.rem(iz + (2 * side - 1) + nz, nz),
        }

    pairs = (
        (gas_in, gas_ref),
        (cell_in, cell_ref),
        (frac_in, frac_ref),
        (tile_in, tile_ref),
        (count_in, count_ref),
        (vel_in, vel_ref),
        (mass_in, mass_ref),
        (temp_in, temp_ref),
    )
    loads = [
        pltpu.make_async_copy(src, dst, load_sem.at[i]) for i, (src, dst) in enumerate(pairs)
    ]
    for load in loads:
        load.start()

    barrier = pltpu.get_barrier_semaphore()
    for k in range(8):
        pl.semaphore_signal(barrier, inc=1, device_id=xy_id(k), device_id_type=MESH)
    z_sides_apart = range(2) if nz > 2 else range(1)
    for side in z_sides_apart:
        for j in range(9):
            pl.semaphore_signal(barrier, inc=1, device_id=z_id(side, j), device_id_type=MESH)

    csend_ref[...] = jnp.zeros_like(csend_ref)
    zsend_ref[...] = jnp.zeros_like(zsend_ref)
    ghost_ref[:, corner_at:, :] = jnp.zeros(
        (comps, ghost_ref.shape[1] - corner_at, cz), F32
    )
    loads[0].wait()
    ysend_ref[0] = gas_ref[:, :, 0, :]
    ysend_ref[1] = gas_ref[:, :, cy - 1, :]
    for j in range(4):
        dx, dy = DIRS[4 + j]
        csend_ref[j, :comps, :] = gas_ref[:, 0 if dx < 0 else cx - 1, 0 if dy < 0 else cy - 1, :]

    def xy_copy(k, base, src, dst):
        return pltpu.make_async_remote_copy(
            src_ref=src,
            dst_ref=dst,
            send_sem=send_sem.at[base + k],
            recv_sem=recv_sem.at[base + OPPOSITE[k]],
            device_id=xy_id(k),
            device_id_type=MESH,
        )

    for c in range(comps):
        turned = gas_ref[c].reshape(plane, cz).T
        lhs_ref[c * cz : (c + 1) * cz, :] = turned.astype(BF16)
        zsend_ref[1, c : c + 1, :] = turned[0:1]
        zsend_ref[0, c : c + 1, :] = turned[cz - 1 : cz]

    def z_copies(base, source, dst):
        copies = []
        for j in range(9):
            for side in z_sides_apart:
                src, at = source(j), OPPOSITE_Z[j]
                apart = len(z_sides_apart) == 2
                copies.append(
                    pltpu.make_async_remote_copy(
                        src_ref=src.at[1 - side] if apart else src,
                        dst_ref=dst.at[at, 1 - side] if apart else dst.at[at],
                        send_sem=send_sem.at[base + 2 * j + side],
                        recv_sem=recv_sem.at[base + 2 * at + (1 - side if apart else 0)],
                        device_id=z_id(side, j),
                        device_id_type=MESH,
                    )
                )
                copies[-1].start()
        return copies

    pl.semaphore_wait(barrier, 8 + 9 * len(z_sides_apart))

    z_halo = z_copies(8, lambda j: zsend_ref, zrecv_ref)
    halo = []
    for k in (4, 5, 6, 7, 0, 1, 2, 3):
        other = OPPOSITE[k]
        if k < 2:
            src = gas_ref.at[:, 0 if k == 0 else cx - 1]
        elif k < 4:
            src = ysend_ref.at[k - 2]
        else:
            src = csend_ref.at[k - 4]
        if k < 4:
            dst = ghost_ref.at[:, pl.ds(starts[other], sizes[other])]
        else:
            dst = crecv_ref.at[other - 4]
        copy = xy_copy(k, 0, src, dst)
        copy.start()
        halo.append(copy)

    for load in loads[1:]:
        load.wait()
    cells = cell_ref[...]
    weight_ref[0] = int_div(cells, TS * cz).astype(F32)
    weight_ref[1] = int_mod(int_div(cells, cz), TS).astype(F32)
    weight_ref[2] = int_mod(cells, cz).astype(F32)
    for axis in range(3):
        offset = frac_ref[axis]
        weight_ref[3 + 3 * axis] = 0.5 * (0.5 - offset) * (0.5 - offset)
        weight_ref[4 + 3 * axis] = 0.75 - offset * offset
        weight_ref[5 + 3 * axis] = 0.5 * (0.5 + offset) * (0.5 + offset)

    tiles_y = cy // TS

    def lane_block(b):
        return pl.ds(pl.multiple_of(b * slots, slots), slots)

    def places(rows, first):
        return (lax.broadcasted_iota(jnp.int32, (rows, slots), 0) + first).astype(F32)

    def ends(length):
        row = lax.broadcasted_iota(jnp.int32, (8, slots), 0)
        return jnp.where(row == 0, 0, jnp.where(row == 1, length + 1, -8)).astype(F32)

    def make_weights(b, carry):
        def row(i):
            return weight_ref[i, pl.ds(b, 1), :]

        tile = tile_ref[b]
        corner_x = (int_div(tile, tiles_y) * TS).astype(F32)
        corner_y = (int_mod(tile, tiles_y) * TS).astype(F32)
        anchor_x, anchor_y, anchor_z = row(0) + corner_x, row(1) + corner_y, row(2)
        tx, ty, tz = [tuple(row(3 + 3 * a + i) for i in range(3)) for a in range(3)]
        wx, wxe = tap(places(cx, 1), anchor_x, *tx), tap(ends(cx), anchor_x, *tx)
        wy, wye = tap(places(cy, 1), anchor_y, *ty), tap(ends(cy), anchor_y, *ty)
        corners = [
            wxe[0 if dx < 0 else 1][None] * wye[0 if dy < 0 else 1][None] for dx, dy in DIRS[4:]
        ]
        planar = jnp.concatenate(
            [
                (wx[:, None, :] * wy[None, :, :]).reshape(plane, slots),
                wxe[0:1] * wy,
                wxe[1:2] * wy,
                wx * wye[0:1],
                wx * wye[1:2],
            ]
            + corners
            + [jnp.zeros((width - plane - corner_at - 4, slots), F32)],
            axis=0,
        )
        at = lane_block(b)
        planar_ref[:, at] = planar.astype(BF16)
        vert_ref[:, at] = tap(places(cz, 1), anchor_z, *tz).astype(BF16)
        vghost_ref[b] = tap(ends(cz), anchor_z, *tz).astype(BF16).astype(F32)
        return carry

    lax.fori_loop(0, blocks, make_weights, 0, unroll=4)

    cell_id = lax.broadcasted_iota(jnp.int32, (plane, LANES), 0)
    ring_id = lax.broadcasted_iota(jnp.int32, (plane, LANES), 1)
    for k in range(8):
        dx, dy = DIRS[k]
        if k < 4:
            step = ring_id - starts[k]
            inside = (step >= 0) & (step < sizes[k])
            if k < 2:
                wanted = step + (cx - 1 if dx < 0 else 0) * cy
            else:
                wanted = step * cy + (cy - 1 if dy < 0 else 0)
        else:
            inside = ring_id == corner_at + k - 4
            wanted = (cx - 1 if dx < 0 else 0) * cy + (cy - 1 if dy < 0 else 0)
        hit = inside & (cell_id == wanted)
        pick_ref[k * plane : (k + 1) * plane, :] = jnp.where(hit, 1.0, 0.0).astype(BF16)

    pair = 2 if blocks % 2 == 0 else 1

    def gather(i, carry):
        at = pl.ds(pl.multiple_of(i * pair * slots, pair * slots), pair * slots)
        planar = planar_ref[:plane, at]
        vertical = vert_ref[:, at].astype(F32)
        near = jnp.dot(lhs_ref[...], planar, preferred_element_type=F32)
        for c in range(comps):
            value = jnp.sum(near[c * cz : (c + 1) * cz] * vertical, axis=0, keepdims=True)
            for j in range(pair):
                gasat_ref[c, pl.ds(i * pair + j, 1), :] = value[:, j * slots : (j + 1) * slots]
        return carry

    lax.fori_loop(0, blocks // pair, gather, 0, unroll=2)

    for copy in halo + z_halo:
        copy.wait_recv()

    for c in range(comps):
        ghost_ref[c, corner_at : corner_at + 4, :] = crecv_ref[:, c, :]
    ring = jnp.concatenate(
        [zrecv_ref[j].reshape(16, plane).astype(BF16) for j in range(8)], axis=1
    )
    ring = jnp.dot(ring, pick_ref[...], preferred_element_type=F32)
    z_values = jnp.concatenate([zrecv_ref[8].reshape(16, plane), ring], axis=1).astype(BF16)

    ghost_rows = ghost_ref[...].reshape(comps * (used - plane), cz).astype(BF16)

    def gather_ghosts(i, carry):
        at = pl.ds(pl.multiple_of(i * pair * slots, pair * slots), pair * slots)
        planar = planar_ref[plane:used, at].astype(F32)
        vertical = vert_ref[:, at]
        near_ends = jnp.dot(z_values, planar_ref[:, at], preferred_element_type=F32)
        low = jnp.concatenate([vghost_ref[i * pair + j, 0:1, :] for j in range(pair)], axis=1)
        high = jnp.concatenate([vghost_ref[i * pair + j, 1:2, :] for j in range(pair)], axis=1)
        both = near_ends[:8] * low + near_ends[8:] * high
        near = jnp.dot(ghost_rows, vertical, preferred_element_type=F32)
        for c in range(comps):
            part = near[c * (used - plane) : (c + 1) * (used - plane)]
            value = jnp.sum(part * planar, axis=0, keepdims=True) + both[c : c + 1]
            for j in range(pair):
                gasat_ref[c, pl.ds(i * pair + j, 1), :] += value[:, j * slots : (j + 1) * slots]
        return carry

    lax.fori_loop(0, blocks // pair, gather_ghosts, 0, unroll=8)

    temper = temp_ref[...]
    diameter = jnp.exp(jnp.log(mass_ref[...]) * (1.0 / 3.0))
    excess = gasat_ref[4] - temper
    spalding = jnp.maximum(excess, 0.0) + jnp.log1p(jnp.exp(-jnp.abs(excess)))
    rate = diameter * jnp.log1p(spalding)
    drag = diameter * gasat_ref[0]
    heat = diameter * excess
    source_ref[0] = rate
    for a in range(3):
        velocity = vel_ref[a]
        source_ref[1 + a] = rate * velocity - drag * (gasat_ref[1 + a] - velocity)
    source_ref[4] = -heat - LATENT * rate

    sghost_ref[...] = jnp.zeros_like(sghost_ref)
    slot_ids = lax.broadcasted_iota(jnp.int32, (1, slots), 1)

    def scale(b, carry):
        at = lane_block(b)
        alive = jnp.where(slot_ids < count_ref[b], PARCEL, 0.0)
        vertical = vert_ref[:, at].astype(F32)
        low, high = vghost_ref[b, 0:1, :], vghost_ref[b, 1:2, :]
        rows = []
        for c in range(comps):
            strength = source_ref[c, pl.ds(b, 1), :] * alive
            scaled_ref[c * cz : (c + 1) * cz, at] = (vertical * strength).astype(BF16)
            rows.append(strength)
        strengths = jnp.concatenate(rows + [jnp.zeros((8 - comps, slots), F32)], axis=0)
        sghost_ref[:, at] = jnp.concatenate([strengths * low, strengths * high], axis=0).astype(BF16)
        return carry

    lax.fori_loop(0, blocks, scale, 0, unroll=4)

    def contract(lhs, rhs):
        return lax.dot_general(lhs, rhs, (((1,), (1,)), ((), ())), preferred_element_type=F32)

    z_ends = contract(sghost_ref[...], planar_ref[...])
    for side in range(2):
        dzsend_ref[0, 1 - side] = z_ends[8 * side : 8 * side + 8, :plane]
        dzsend_ref[1, 1 - side] = z_ends[8 * side : 8 * side + 8, plane:]
    z_deposit = z_copies(34, lambda j: dzsend_ref.at[0 if j == 8 else 1], dzrecv_ref)

    dcsend_ref[...] = jnp.zeros_like(dcsend_ref)
    all_ghosts = contract(planar_ref[plane:used, :], scaled_ref[...])
    for c in range(comps):
        ghosts = all_ghosts[:, c * cz : (c + 1) * cz]
        dep_ref[c] = ghosts
        for j in range(4):
            dcsend_ref[j, c : c + 1, :] = ghosts[corner_at + j : corner_at + j + 1]

    deposit = []
    for k in (4, 5, 6, 7, 0, 1, 2, 3):
        other = OPPOSITE[k]
        if k < 4:
            src = dep_ref.at[:, pl.ds(starts[k], sizes[k])]
            dst = (dxrecv_ref if k < 2 else dyrecv_ref).at[other % 2]
        else:
            src, dst = dcsend_ref.at[k - 4], dcrecv_ref.at[other - 4]
        copy = xy_copy(k, 26, src, dst)
        copy.start()
        deposit.append(copy)

    lane = lax.broadcasted_iota(jnp.int32, (plane, cz), 1)
    row_y = int_mod(lax.broadcasted_iota(jnp.int32, (plane, cz), 0), cy)

    def columns(ref):
        both = ref[8].reshape(16, plane)
        return jnp.concatenate([both, jnp.zeros((LANES - 16, plane), F32)], axis=0).T

    def at_ends(turned, first, rows, at):
        lanes = lax.broadcasted_iota(jnp.int32, (rows, cz), 1)
        low = turned[first : first + rows, at : at + 1]
        high = turned[first : first + rows, 8 + at : 9 + at]
        return jnp.where(lanes == 0, low, 0.0) + jnp.where(lanes == cz - 1, high, 0.0)

    z_sides = columns(zrecv_ref)
    all_own = contract(planar_ref[:plane, :], scaled_ref[...])
    flow = [gas_ref[1 + a].reshape(plane, cz) for a in range(3)]
    for c in range(comps):
        cube = gas_ref[c]
        q = cube.reshape(plane, cz)
        x_low = jnp.concatenate([ghost_ref[c, 0:cy], q[: plane - cy]], axis=0)
        x_high = jnp.concatenate([q[cy:], ghost_ref[c, cy : 2 * cy]], axis=0)

        def edge(first):
            ghost = ghost_ref[c, first : first + cx]
            return jnp.broadcast_to(ghost[:, None, :], (cx, cy, cz)).reshape(plane, cz)

        y_low = jnp.where(row_y == 0, edge(2 * cy), pltpu.roll(q, 1, 0))
        y_high = jnp.where(row_y == cy - 1, edge(2 * cy + cx), pltpu.roll(q, plane - 1, 0))
        z_low = jnp.where(lane == 0, z_sides[:, c : c + 1], pltpu.roll(q, 1, 1))
        z_high = jnp.where(lane == cz - 1, z_sides[:, 8 + c : 9 + c], pltpu.roll(q, cz - 1, 1))
        laplace = -6.0 * q + x_high + x_low + y_high + y_low + z_high + z_low
        advect = 0.5 * (
            flow[0] * (x_high - x_low) + flow[1] * (y_high - y_low) + flow[2] * (z_high - z_low)
        )
        own = all_own[:, c * cz : (c + 1) * cz]
        out_ref[c] = (q + TIME_INCREMENT * (VISCOSITY * laplace - advect + own)).reshape(cx, cy, cz)

    for copy in z_deposit + deposit:
        copy.wait_recv()

    inner = columns(dzrecv_ref)
    outer = jnp.concatenate([dzrecv_ref[j].reshape(16, LANES) for j in range(8)], axis=0).T
    for c in range(comps):
        ends_c = at_ends(inner, 0, plane, c)
        out_ref[c] += TIME_INCREMENT * ends_c.reshape(cx, cy, cz)
        for side in range(2):
            x_at, y_at = (cx - 1) * side, (cy - 1) * side
            x_ends = at_ends(outer, starts[1 - side], cy, 16 * side + c)
            y_ends = at_ends(outer, starts[3 - side], cx, 16 * (2 + side) + c)
            out_ref[c, x_at] += TIME_INCREMENT * (dxrecv_ref[side, c] + x_ends)
            out_ref[c, :, y_at, :] += TIME_INCREMENT * (dyrecv_ref[side, c] + y_ends)
        for j in range(4):
            dx, dy = DIRS[4 + j]
            x_at, y_at = 0 if dx < 0 else cx - 1, 0 if dy < 0 else cy - 1
            corner = at_ends(outer, corner_at + OPPOSITE[4 + j] - 4, 1, 16 * (4 + j) + c)
            out_ref[c, x_at, y_at : y_at + 1, :] += TIME_INCREMENT * (
                dcrecv_ref[j, c : c + 1, :] + corner
            )

    for copy in halo + z_halo + z_deposit + deposit:
        copy.wait_send()


def local(
    gas_state,
    section_start,
    drop_cell,
    block_tile,
    droplets_per_block,
    drop_frac,
    drop_vel,
    drop_mass,
    drop_temp,
):
    comps, cx, cy, cz = gas_state.shape
    blocks, slots = drop_cell.shape[3:]
    plane = cx * cy
    ghosts = 2 * cx + 2 * cy + 4
    ghost_width = -(-ghosts // LANES) * LANES
    width = plane + ghost_width
    used = plane + -(-ghosts // 16) * 16
    total = blocks * slots
    vmem = pl.BlockSpec(memory_space=pltpu.VMEM)
    section = pl.pallas_call(
        kernel,
        out_shape=pltpu.VMEM(gas_state.shape, F32),
        in_specs=[pl.BlockSpec(memory_space=pl.ANY)] * 8,
        out_specs=vmem,
        scratch_shapes=[
            pltpu.SMEM((blocks,), jnp.int32),
            pltpu.SMEM((blocks,), jnp.int32),
            pltpu.VMEM(gas_state.shape, F32),
            pltpu.VMEM((blocks, slots), jnp.int32),
            pltpu.VMEM((3, blocks, slots), F32),
            pltpu.VMEM((3, blocks, slots), F32),
            pltpu.VMEM((blocks, slots), F32),
            pltpu.VMEM((blocks, slots), F32),
            pltpu.VMEM((8 * plane, ghost_width), BF16),
            pltpu.VMEM((12, blocks, slots), F32),
            pltpu.VMEM((width, total), BF16),
            pltpu.VMEM((cz, total), BF16),
            pltpu.VMEM((blocks, 8, slots), F32),
            pltpu.VMEM((comps * cz, total), BF16),
            pltpu.VMEM((16, total), BF16),
            pltpu.VMEM((comps * cz, plane), BF16),
            pltpu.VMEM((comps, used - plane, cz), F32),
            pltpu.VMEM((2, comps, cx, cz), F32),
            pltpu.VMEM((4, 8, cz), F32),
            pltpu.VMEM((4, 8, cz), F32),
            pltpu.VMEM((2, 8, plane), F32),
            pltpu.VMEM((9, 2, 8, plane), F32),
            pltpu.VMEM((comps, blocks, slots), F32),
            pltpu.VMEM((comps, blocks, slots), F32),
            pltpu.VMEM((comps, used - plane, cz), F32),
            pltpu.VMEM((4, 8, cz), F32),
            pltpu.VMEM((2, 2, 8, ghost_width), F32),
            pltpu.VMEM((9, 2, 8, ghost_width), F32),
            pltpu.VMEM((2, comps, cy, cz), F32),
            pltpu.VMEM((2, comps, cx, cz), F32),
            pltpu.VMEM((4, 8, cz), F32),
            pltpu.SemaphoreType.DMA((8,)),
            pltpu.SemaphoreType.DMA((52,)),
            pltpu.SemaphoreType.DMA((52,)),
        ],
        compiler_params=pltpu.CompilerParams(collective_id=0, has_side_effects=True),
    )(
        block_tile.reshape(block_tile.shape[3:]),
        droplets_per_block.reshape(droplets_per_block.shape[3:]),
        gas_state,
        drop_cell.reshape(drop_cell.shape[3:]),
        drop_frac.reshape(drop_frac.shape[3:]),
        drop_vel.reshape(drop_vel.shape[3:]),
        drop_mass.reshape(drop_mass.shape[3:]),
        drop_temp.reshape(drop_temp.shape[3:]),
    )
    return 0.75 * section_start + 0.25 * section


def solution(mesh):
    in_specs = (
        P(None, "gx", "gy", "gz"),
        P(None, "gx", "gy", "gz"),
        P("gx", "gy", "gz", None, None),
        P("gx", "gy", "gz", None),
        P("gx", "gy", "gz", None),
        P("gx", "gy", "gz", None, None, None),
        P("gx", "gy", "gz", None, None, None),
        P("gx", "gy", "gz", None, None),
        P("gx", "gy", "gz", None, None),
    )
    out_specs = P(None, "gx", "gy", "gz")
    return jax.shard_map(local, mesh=mesh, in_specs=in_specs, out_specs=out_specs, check_vma=False)
```
